32 devices in a mesh: groups: 2 (over y), seq: 4 (over z), head: 2 (over x), sub: 2 (over core).
Axes of the slice: x: 2, y: 2, z: 4, core: 2. Of those that a mesh axis runs over, the one named last changes fastest.
Arguments:
- wave_pieces: float32 [8, 2, 2, 64, 3072], P(('groups', 'seq'), 'head', 'sub'), parts along dimension 0, may hold values from -6 to 6
- piece_target: int32 [8, 2, 2, 64], P(('groups', 'seq'), 'head', 'sub'), parts along dimension 0, may hold values from -1 to 127, as said below
- utt_lengths: int32 [8], P('groups'), parts along dimension 0, may hold values from 1 to 1088, 2176 in all
- sub_weight: bfloat16 [512, 1536], P(None, 'head'), may hold values from -2 to 2
- sub_bias: bfloat16 [1536], P('head'), may hold values from -4 to 4
- norm_gain: float32 [1536], replicated, may hold values from 0.1 to 1.9
- qkv_weight: bfloat16 [1536, 3, 1536], P(None, None, 'head'), may hold values from -0.21875 to 0.21875
- rel_bias: float32 [24, 543], P('head'), may hold values from -4 to 250
Outputs:
- context: bfloat16 [4352, 1536], P(('groups', 'seq', 'sub'), 'head'), parts along dimension 0
The draws below stay inside these ranges and needn't reach their ends.
There are 2 independent parts, one for each index of `groups`. The reference program is written for one: setup_inputs(seed, part) draws one part's arguments, and reference() takes and returns one part's arrays. A program takes and returns all parts, laid end to end along the dimension named above; an argument that names none is the same for every part. Nothing has to cross between parts.
Inputs may be any that keep to these rules, and one draw needn't show every extreme that they name: `piece_target`: each value is -1 (an empty slot) or s * 32 + p, naming piece p of seq index s for the loader's own head and sub indices. Every piece of every eighth is named by exactly one slot of a loader with the same head and sub indices. A loader names at most 16 pieces of one seq index; in every draw some loaders name exactly 16 pieces of every seq index, so that all their slots are full.
All inputs are finite; a program needn't handle non-finite values.
Results may differ from the reference program's by a relative error of at most 0.006.
Values may be sent and summed in bfloat16 or wider, within the bound.
A program may use at most 64 MiB of HBM per device.

```python
import math
import jax
import jax.numpy as jnp
import numpy as np
from jax import lax

D = 1536
HEADS = 24
HDIM = 64
MEL = 128
NFFT = 512
HOP = 160
FP = 17
CH = 136
PE = 32
PL = 3072
BINS = 257
CAP = 16
LOAD = 64
HEAVY = 1
HALF_TOK = 272
TOKENS = 2176
UTTS = 4
UTT_MOST = 1088
N_SEQ = 4
N_HEAD = 2
N_SUB = 2


def draw_wave_pieces(key, part):
    key_noise, key_gain = jax.random.split(jax.random.fold_in(key, 3))
    shape = (N_SEQ, N_HEAD, N_SUB, LOAD, PL)
    gains = jnp.exp(jax.random.uniform(key_gain, (N_SEQ, N_HEAD, N_SUB, LOAD, 1), jnp.float32, math.log(0.1), 0.0))
    noise = jnp.clip(jax.random.normal(key_noise, shape, jnp.float32), -6.0, 6.0)
    return (noise * gains).astype(jnp.float32)


def column_plan(key):
    key_heavy, key_extra, key_place, key_order = jax.random.split(key, 4)
    heavy_rank = jax.random.permutation(key_heavy, N_SEQ)
    is_heavy = heavy_rank < HEAVY
    light_total = PE - HEAVY * CAP
    light_loaders = N_SEQ - HEAVY
    light_base = light_total // light_loaders
    light_extra = light_total % light_loaders
    priority = jax.vmap(lambda sub_key: jax.random.permutation(sub_key, N_SEQ))(jax.random.split(key_extra, N_SEQ))
    ahead = (priority[:, None, :] < priority[:, :, None]) & jnp.logical_not(is_heavy)[None, None, :]
    light_rank = jnp.sum(ahead.astype(jnp.int32), axis=2)
    counts = jnp.where(is_heavy[None, :], CAP, light_base + (light_rank < light_extra).astype(jnp.int32))
    offsets = jnp.cumsum(counts, axis=1) - counts
    placement = jax.vmap(lambda sub_key: jax.random.permutation(sub_key, PE))(jax.random.split(key_place, N_SEQ))
    slot_number = jnp.arange(LOAD)
    slot_shard = slot_number // CAP
    slot_rank = slot_number % CAP
    live = slot_rank[None, :] < jnp.transpose(counts)[:, slot_shard]
    order_index = jnp.minimum(jnp.transpose(offsets)[:, slot_shard] + slot_rank[None, :], PE - 1)
    position = placement[slot_shard[None, :], order_index]
    targets = jnp.where(live, slot_shard[None, :] * PE + position, -1)
    shuffles = jax.vmap(lambda sub_key: jax.random.permutation(sub_key, LOAD))(jax.random.split(key_order, N_SEQ))
    return jnp.take_along_axis(targets, shuffles, axis=1).astype(jnp.int32)


def draw_piece_target(key, part):
    column_keys = jax.random.split(jax.random.fold_in(key, 11), N_HEAD * N_SUB)
    per_column = jax.vmap(column_plan)(column_keys)
    return jnp.transpose(per_column.reshape(N_HEAD, N_SUB, N_SEQ, LOAD), (2, 0, 1, 3)).astype(jnp.int32)


def draw_sub_weight(key, part):
    key_values, key_scale = jax.random.split(jax.random.fold_in(key, 7))
    column_scale = jnp.exp(jax.random.uniform(key_scale, (1, D), jnp.float32, math.log(0.3), math.log(3.0)))
    values = jnp.clip(jax.random.normal(key_values, (4 * MEL, D), jnp.float32), -4.0, 4.0)
    return (values * column_scale * (1.0 / math.sqrt(4 * MEL))).astype(jnp.bfloat16)


def draw_rel_bias(key, part):
    width = 4 * CH - 1
    key_values = jax.random.fold_in(key, 5)
    values = jnp.clip(jax.random.normal(key_values, (HEADS, width), jnp.float32), -4.0, 4.0)
    return values.astype(jnp.float32)


def shard_levels(own_key, shape, shards, low, high):
    def one(axis_at, blocks):
        heights = jax.random.uniform(jax.random.fold_in(jax.random.fold_in(own_key, 6), axis_at), (blocks,), jnp.float32, low / len(shards), high / len(shards))
        return jnp.repeat(jnp.exp(heights), shape[axis_at] // blocks).reshape((-1,) + (1,) * (len(shape) - axis_at - 1))

    level = one(*shards[0])
    for cut in shards[1:]:
        level = level * one(*cut)
    return level


def length_profile(amount, total, limit, slope):
    portions = [(1 << 20) // math.isqrt(standing ** slope) + 1 for standing in range(2, amount + 1)]
    rest, given = total - limit - (amount - 1), [1] * (amount - 1)
    while rest > 0:
        free = [i for i in range(amount - 1) if given[i] < limit]
        pool, remaining = sum([portions[i] for i in free]), rest
        for i in free:
            more = min(limit - given[i], max(1, remaining * portions[i] // pool), rest)
            given[i] = given[i] + more
            rest = rest - more
    return np.array([limit] + given)


def ragged(rng, count, total, bound, lean):
    if count == 2:
        one = jax.random.randint(rng, (), max(1, total - bound), min(bound, total - 1) + 1)
        return jnp.stack([one, total - one])
    sizes = jnp.asarray(length_profile(count, total, bound, lean), jnp.int32)
    twos = (count - 1) // 2
    source_of, taker = sizes[1:1 + 2 * twos:2], sizes[2:2 + 2 * twos:2]
    margin = jnp.minimum(source_of - 1, bound - taker)
    shifted = jax.random.randint(jax.random.fold_in(rng, 1), (twos,), 0, 1 << 20) % (margin + 1)
    sizes = sizes.at[1:1 + 2 * twos:2].set(source_of - shifted).at[2:2 + 2 * twos:2].set(taker + shifted)
    return sizes[jax.random.permutation(jax.random.fold_in(rng, 2), count)]


def normal_values(key, dims, deviation, bound, pieces=(), held_as=jnp.bfloat16):
    array = deviation * jax.random.normal(key, dims, jnp.float32)
    if pieces:
        array = array * shard_levels(key, dims, pieces, -0.22, 0.18)
    return jnp.clip(array, -bound, bound).astype(held_as)


def setup_inputs(seed: int = 0, part: int = 0) -> dict:
    arg_keys = jax.random.split(jax.random.key(seed), 9)
    part_keys = jax.random.split(jax.random.fold_in(arg_keys[8], part), 9)
    wave_pieces = draw_wave_pieces(jax.random.fold_in(jax.random.fold_in(arg_keys[8], part), 71), part)
    piece_target = draw_piece_target(jax.random.fold_in(jax.random.fold_in(arg_keys[8], part), 71), part)
    utt_lengths = ragged(part_keys[2], UTTS, TOKENS, UTT_MOST, 2).astype(jnp.int32)
    sub_weight = draw_sub_weight(jax.random.fold_in(arg_keys[8], 71), part)
    sub_bias = normal_values(arg_keys[4], (D,), 1.0, 4.0, ((0, 2),))
    norm_gain = jnp.clip(1.0 + 0.18 * jax.random.normal(arg_keys[5], (D,), jnp.float32), 0.1, 1.9)
    qkv_weight = normal_values(arg_keys[6], (D, 3, D), (D // 2) ** -0.5, 0.21875, ((2, 2),))
    rel_bias = draw_rel_bias(jax.random.fold_in(arg_keys[8], 71), part)
    return {"wave_pieces": wave_pieces, "piece_target": piece_target, "utt_lengths": utt_lengths, "sub_weight": sub_weight, "sub_bias": sub_bias, "norm_gain": norm_gain, "qkv_weight": qkv_weight, "rel_bias": rel_bias}


SAMPLE_RATE = 16000.0
EPSILON = 1e-05
MASKED = -1e+30

def window_table():
    sample_index = jnp.arange(NFFT).astype(jnp.float32)
    return 0.5 - 0.5 * jnp.cos(2.0 * math.pi / NFFT * sample_index)

def fourier_table():
    sample_index = jnp.arange(NFFT).astype(jnp.int32)[:, None]
    bin_index = jnp.arange(BINS).astype(jnp.int32)[None, :]
    phase = (sample_index * bin_index % NFFT).astype(jnp.float32) * (2.0 * math.pi / NFFT)
    return jnp.concatenate([jnp.cos(phase), jnp.sin(phase)], axis=1)

def mel_table():
    highest = 2595.0 * math.log10(1.0 + SAMPLE_RATE / 2.0 / 700.0)
    points = jnp.arange(MEL + 2).astype(jnp.float32) * (highest / (MEL + 1))
    hertz = 700.0 * (jnp.power(10.0, points / 2595.0) - 1.0)
    centres = jnp.arange(BINS).astype(jnp.float32) * (SAMPLE_RATE / NFFT)
    rising = (centres[:, None] - hertz[None, :-2]) / (hertz[1:-1] - hertz[:-2])[None, :]
    falling = (hertz[None, 2:] - centres[:, None]) / (hertz[2:] - hertz[1:-1])[None, :]
    return jnp.maximum(0.0, jnp.minimum(rising, falling))

def log_mel(piece_rows):
    piece_count = piece_rows.shape[0]
    frames = jnp.stack([piece_rows[:, HOP * frame_index:HOP * frame_index + NFFT] for frame_index in range(FP)], axis=1)
    frames = frames * window_table()[None, None, :]
    spectra = jnp.dot(frames.reshape(piece_count * FP, NFFT), fourier_table(), precision=lax.Precision.HIGHEST)
    power_bins = spectra[:, :BINS] * spectra[:, :BINS] + spectra[:, BINS:] * spectra[:, BINS:]
    energy = jnp.dot(power_bins, mel_table(), precision=lax.Precision.HIGHEST)
    return jnp.log(1.0 + energy).astype(jnp.bfloat16).reshape(piece_count, FP * MEL)

def reference(wave_pieces, piece_target, utt_lengths, sub_weight, sub_bias, norm_gain, qkv_weight, rel_bias):
    column_count = N_HEAD * N_SUB
    slot_rows = jnp.transpose(wave_pieces, (1, 2, 0, 3, 4)).reshape(column_count, N_SEQ * LOAD, PL)
    targets = jnp.transpose(piece_target, (1, 2, 0, 3)).reshape(column_count, N_SEQ * LOAD).astype(jnp.int32)
    targets = jnp.where(targets < 0, N_SEQ * PE, targets).astype(jnp.int32)

    def place(column_rows, slot_goals):
        return jnp.zeros((N_SEQ * PE, PL), jnp.float32).at[slot_goals].set(column_rows.astype(jnp.float32), mode='drop')
    placed = jax.vmap(place)(slot_rows, targets)
    placed = jnp.transpose(placed.reshape(N_HEAD, N_SUB, N_SEQ, PE, PL), (2, 1, 0, 3, 4))

    def shard_mel(shard_pieces):
        return log_mel(shard_pieces.reshape(N_SUB * N_HEAD * PE, PL))
    mel_pieces = lax.map(shard_mel, placed)
    token_rows = mel_pieces.reshape(TOKENS, 4 * MEL)
    features = jax.nn.silu(jnp.dot(token_rows, sub_weight, preferred_element_type=jnp.float32) + sub_bias.astype(jnp.float32)).astype(jnp.bfloat16)

    def project(half_rows):
        values = half_rows.astype(jnp.float32)
        centred = values - lax.optimization_barrier(jnp.mean(values, axis=1, keepdims=True))
        variance = lax.optimization_barrier(jnp.mean(centred * centred, axis=1, keepdims=True))
        normed = (centred * lax.rsqrt(variance + EPSILON) * norm_gain[None, :]).astype(jnp.bfloat16)
        return jnp.dot(normed, qkv_weight.reshape(D, 3 * D), preferred_element_type=jnp.float32).astype(jnp.bfloat16)
    projected = lax.map(project, features.reshape(N_SEQ * N_SUB, HALF_TOK, D)).reshape(TOKENS, 3, HEADS, HDIM)
    queries = projected[:, 0]
    padding = jnp.zeros((CH, HEADS, HDIM), jnp.bfloat16)
    key_padded = jnp.concatenate([padding, projected[:, 1], padding], axis=0)
    value_padded = jnp.concatenate([padding, projected[:, 2], padding], axis=0)
    utterance_ends = jnp.cumsum(utt_lengths).astype(jnp.int32)
    positions = (jnp.arange(TOKENS + 2 * CH) - CH).astype(jnp.int32)
    utterance_ids = lax.optimization_barrier(jnp.sum((utterance_ends[None, :] <= positions[:, None]).astype(jnp.int32), axis=1)).astype(jnp.int32)
    key_inside = (positions >= 0) & (positions < TOKENS)
    relative_index = (jnp.arange(CH)[:, None] - jnp.arange(3 * CH)[None, :] + 3 * CH - 1).astype(jnp.int32)
    position_bias = rel_bias[:, relative_index]

    def attend(block_index):
        start = (block_index * CH).astype(jnp.int32)
        query_block = lax.dynamic_slice_in_dim(queries, start, CH, 0).astype(jnp.float32)
        key_block = lax.dynamic_slice_in_dim(key_padded, start, 3 * CH, 0).astype(jnp.float32)
        value_block = lax.dynamic_slice_in_dim(value_padded, start, 3 * CH, 0).astype(jnp.float32)
        query_utt = lax.dynamic_slice_in_dim(utterance_ids, start + CH, CH, 0)
        key_utt = lax.dynamic_slice_in_dim(utterance_ids, start, 3 * CH, 0)
        key_valid = lax.dynamic_slice_in_dim(key_inside, start, 3 * CH, 0)
        scores = jnp.einsum('qhd,khd->hqk', query_block, key_block) * (1.0 / math.sqrt(HDIM)) + position_bias
        allowed = (query_utt[:, None] == key_utt[None, :]) & key_valid[None, :]
        scores = jnp.where(allowed[None, :, :], scores, MASKED)
        row_peak = lax.optimization_barrier(jnp.max(scores, axis=2, keepdims=True))
        weights = jnp.exp(scores - row_peak)
        attention_weights = (weights / lax.optimization_barrier(jnp.sum(weights, axis=2, keepdims=True))).astype(jnp.bfloat16)
        context = jnp.einsum('hqk,khd->qhd', attention_weights.astype(jnp.float32), value_block)
        return context.astype(jnp.bfloat16).reshape(CH, D)
    contexts = lax.map(attend, jnp.arange(TOKENS // CH).astype(jnp.int32))
    return contexts.reshape(TOKENS, D)
```

```python
import functools
import math

import jax
import jax.numpy as jnp
import numpy as np
from jax import lax
from jax.experimental import pallas as pl
from jax.experimental.pallas import tpu as pltpu
from jax.sharding import PartitionSpec as P

HDIM = 64
MEL = 128
NFFT = 512
HOP = 160
FP = 17
CH = 136
PE = 32
LANES = 128
TABLE = 640
KEYS = 512
ROWS = 144


SAMPLE_RATE = 16000.0
EPSILON = 1e-05
MASKED = -1e30
MESH = pl.DeviceIdType.MESH


def split_bf16(table):
    high = table.astype(np.float32).astype(jnp.bfloat16)
    low = (table - high.astype(np.float64)).astype(np.float32).astype(jnp.bfloat16)
    return np.stack([high, low])


def stacked(table):
    high, low = split_bf16(table)
    return np.concatenate([high, high, low], axis=0)


def window_table():
    return (0.5 - 0.5 * np.cos(2.0 * np.pi / NFFT * np.arange(NFFT)))[None].astype(np.float32)


def fourier_tables():
    half = NFFT // 2
    sample = np.arange(half)[:, None]

    def phase(bins):
        return (sample * bins[None, :] % NFFT) * (2.0 * np.pi / NFFT)

    even, odd = np.arange(0, half, 2), np.arange(1, half, 2)
    even_sine = np.sin(phase(even))
    even_sine[:, 0] = np.cos(phase(np.array([half])))[:, 0]
    even_table = np.concatenate([np.cos(phase(even)), even_sine], axis=1)
    odd_table = np.concatenate([np.cos(phase(odd)), np.sin(phase(odd))], axis=1)
    return np.stack([stacked(even_table), stacked(odd_table)])


def mel_table():
    bin_total = NFFT // 2 + 1
    highest = 2595.0 * math.log10(1.0 + SAMPLE_RATE / 2.0 / 700.0)
    points = np.arange(MEL + 2) * (highest / (MEL + 1))
    hertz = 700.0 * (np.power(10.0, points / 2595.0) - 1.0)
    centres = np.arange(bin_total) * (SAMPLE_RATE / NFFT)
    rising = (centres[:, None] - hertz[None, :-2]) / (hertz[1:-1] - hertz[:-2])[None, :]
    falling = (hertz[None, 2:] - centres[:, None]) / (hertz[2:] - hertz[1:-1])[None, :]
    table = np.maximum(0.0, np.minimum(rising, falling))
    sine_even = table[0 : bin_total - 1 : 2].copy()
    sine_even[0] = table[bin_total - 1]
    rows = np.concatenate(
        [table[0 : bin_total - 1 : 2], sine_even, table[1::2], table[1::2]], axis=0
    )
    return rows.astype(np.float32).astype(jnp.bfloat16)


def dot(left, right):
    return jnp.dot(left, right, preferred_element_type=jnp.float32)


def dot_split(value, table):
    value_high = value.astype(jnp.bfloat16)
    value_low = (value - value_high.astype(jnp.float32)).astype(jnp.bfloat16)
    return dot(jnp.concatenate([value_high, value_low, value_high], axis=1), table)


def groups_of(shift):
    return range((FP - shift + 3) // 4)


def front_kernel(
    shards, heads, subs,
    wave_in, target_in, weight_ref, window_in, fourier_in, mel_in, sub_bias_in, gain_in, rel_in,
    qkv_in, lengths_in,
    queries_ref, keys_ref, values_ref, bias_ref,
    wave_ref, target_ref, window_ref, fourier_ref, mel_ref, sub_bias_row, gain_row, rel_ref,
    weights_ref, sub_bias_ref, qkv_ref, lengths_ref, spread_ref,
    packed_0, packed_1, packed_2, packed_3, received_0, received_1, received_2, received_3,
    frames_0, frames_1, frames_2, frames_3,
    lsem, wsend, wrecv, fsend, frecv, asend, arecv, hsend, hrecv, nsend, nrecv, bsend, brecv,
):
    s, h, u = lax.axis_index("seq"), lax.axis_index("head"), lax.axis_index("sub")
    half = s * subs + u
    halves = shards * subs
    slots = wave_ref.shape[0]
    cap = slots // shards
    depth = weight_ref.shape[0] // subs

    packed = (packed_0, packed_1, packed_2, packed_3)
    received = (received_0, received_1, received_2, received_3)
    frames = (frames_0, frames_1, frames_2, frames_3)

    def place_of(index):
        return {"seq": index // subs, "sub": index % subs}

    def when(condition, action):
        @pl.when(condition)
        def _():
            action()

    pairs = (
        (target_in, target_ref), (wave_in, wave_ref), (window_in, window_ref),
        (fourier_in, fourier_ref), (mel_in, mel_ref), (sub_bias_in, sub_bias_row),
        (gain_in, gain_row), (rel_in, rel_ref), (lengths_in, lengths_ref),
        (weight_ref, weights_ref.at[h]),
        (qkv_in.at[0], qkv_ref.at[0]), (qkv_in.at[1], qkv_ref.at[1]),
        (qkv_in.at[2], qkv_ref.at[2]),
    )
    loads = [pltpu.make_async_copy(a, b, lsem.at[i]) for i, (a, b) in enumerate(pairs)]
    for load in loads[:9]:
        load.start()

    barrier = pltpu.get_barrier_semaphore()
    for d in range(1, shards):
        pl.semaphore_signal(
            barrier, inc=1, device_id={"seq": lax.rem(s + d, shards)}, device_id_type=MESH
        )
    for d in range(1, heads):
        pl.semaphore_signal(
            barrier, inc=1, device_id={"head": lax.rem(h + d, heads)}, device_id_type=MESH
        )

    @pl.when(half > 0)
    def _():
        pl.semaphore_signal(barrier, inc=1, device_id=place_of(half - 1), device_id_type=MESH)

    @pl.when(half < halves - 1)
    def _():
        pl.semaphore_signal(barrier, inc=1, device_id=place_of(half + 1), device_id_type=MESH)

    inner = jnp.where(half > 0, 1, 0) + jnp.where(half < halves - 1, 1, 0)
    pl.semaphore_wait(barrier, shards - 1 + heads - 1 + inner)

    weight_copies, bias_copies = [], []
    for d in range(1, heads):
        copy = pltpu.make_async_remote_copy(
            src_ref=weight_ref.at[pl.ds(u * depth, depth)],
            dst_ref=weights_ref.at[h, pl.ds(u * depth, depth)],
            send_sem=wsend.at[d - 1],
            recv_sem=wrecv.at[d - 1],
            device_id={"head": lax.rem(h + d, heads)},
            device_id_type=MESH,
        )
        copy.start()
        weight_copies.append(copy)

    loads[0].wait()
    target = target_ref[...]
    owner = jnp.where(target >= 0, lax.shift_right_arithmetic(target, 5), shards)
    place = jnp.bitwise_and(target, PE - 1)
    down = lax.broadcasted_iota(jnp.int32, (slots, slots), 0)
    across = lax.broadcasted_iota(jnp.int32, (slots, slots), 1)
    owner_wide = jnp.broadcast_to(owner, (slots, slots))
    owner_down = jnp.sum(jnp.where(down == across, owner_wide, 0), axis=1, keepdims=True)
    rank = jnp.sum(
        jnp.where((owner_down == owner_wide) & (down < across), 1, 0), axis=0, keepdims=True
    )
    goal = jnp.where(owner < shards, owner * cap + rank, -1)
    chosen = down == goal
    select = chosen.astype(jnp.float32).astype(jnp.bfloat16)
    code = jnp.sum(jnp.where(chosen, place + 1, 0), axis=1, keepdims=True).astype(jnp.float32)
    code = jnp.broadcast_to(code, (slots, LANES)).astype(jnp.bfloat16)

    piece_copies = []
    for index in range(1, 5):
        loads[index].wait()
    for load in loads[9:]:
        load.start()
    for shift in range(4):
        wave = wave_ref[...]
        if shift:
            wave = pltpu.roll(wave, wave.shape[1] - 32 * shift, 1)
        groups = groups_of(shift)
        pieces = [
            wave[:, LANES * (5 * g + shift) : LANES * (5 * g + shift) + NFFT] * window_ref[...]
            for g in groups
        ]
        pieces = jnp.concatenate(pieces, axis=0)
        low, high = pieces[:, : NFFT // 2], pieces[:, NFFT // 2 :]
        even = dot_split(low + high, fourier_ref[0])
        odd = dot_split(low - high, fourier_ref[1])
        squares = jnp.concatenate([even * even, odd * odd], axis=1).astype(jnp.bfloat16)
        energy = dot(squares, mel_ref[...])
        logs = jnp.log(1.0 + energy).astype(jnp.bfloat16)
        logs = jnp.concatenate([logs[g * slots : (g + 1) * slots] for g in groups], axis=1)
        rows = dot(select, logs).astype(jnp.bfloat16)
        wide = len(groups) * MEL
        for t in range(shards):
            packed[shift][t, :, :wide] = rows[t * cap : (t + 1) * cap]
            if shift == 0:
                packed[0][t, :, wide:] = code[t * cap : (t + 1) * cap]
        for d in range(1, shards):
            to = lax.rem(s + d, shards)
            copy = pltpu.make_async_remote_copy(
                src_ref=packed[shift].at[to],
                dst_ref=received[shift].at[s],
                send_sem=asend.at[shift, d - 1],
                recv_sem=arecv.at[shift, d - 1],
                device_id={"seq": to},
                device_id_type=MESH,
            )
            copy.start()
            piece_copies.append(copy)
        received[shift][s] = packed[shift][s]

    loads[5].wait()
    sub_bias_ref[h] = sub_bias_row[...].astype(jnp.float32).reshape(1, sub_bias_row.shape[0])
    for d in range(1, heads):
        copy = pltpu.make_async_remote_copy(
            src_ref=sub_bias_ref.at[h],
            dst_ref=sub_bias_ref.at[h],
            send_sem=bsend.at[d - 1],
            recv_sem=brecv.at[d - 1],
            device_id={"head": lax.rem(h + d, heads)},
            device_id_type=MESH,
        )
        copy.start()
        bias_copies.append(copy)

    @pl.when(half == 0)
    def _():
        for shift in range(4):
            frames[shift][0] = jnp.zeros(frames[shift].shape[1:], jnp.bfloat16)

    @pl.when(half == halves - 1)
    def _():
        for shift in range(4):
            frames[shift][heads + 1] = jnp.zeros(frames[shift].shape[1:], jnp.bfloat16)

    for slot in range(spread_ref.shape[0]):
        spread_ref[slot, PE * FP :] = jnp.zeros((4 * ROWS - PE * FP, MEL), jnp.float32)

    loads[6].wait()
    loads[7].wait()
    loads[8].wait()
    first_token, token_total = half * heads * CH, halves * heads * CH
    masks = []
    for b in range(heads):
        query_pos = first_token + b * CH + lax.broadcasted_iota(jnp.int32, (CH, 1), 0)
        key_index = lax.broadcasted_iota(jnp.int32, (1, KEYS), 1)
        key_pos = first_token + (b - 1) * CH + key_index
        end = jnp.int32(0)
        query_utt = jnp.zeros_like(query_pos)
        key_utt = jnp.zeros_like(key_pos)
        for r in range(lengths_ref.shape[0]):
            end = end + lengths_ref[r]
            query_utt = query_utt + (query_pos >= end).astype(jnp.int32)
            key_utt = key_utt + (key_pos >= end).astype(jnp.int32)
        inside = (key_pos >= 0) & (key_pos < token_total) & (key_index < 3 * CH)
        key_utt = jnp.where(inside, key_utt, -1)
        masks.append(jnp.where(query_utt == key_utt, 0.0, MASKED))
    taps = rel_ref.shape[1]
    mirror = lax.broadcasted_iota(jnp.int32, (taps, TABLE), 0) + lax.broadcasted_iota(
        jnp.int32, (taps, TABLE), 1
    )
    mirror = (mirror == taps - 1).astype(jnp.float32).astype(jnp.bfloat16)
    rest = rel_ref[...]
    terms = []
    for _ in range(3):
        term = rest.astype(jnp.bfloat16)
        rest = rest - term.astype(jnp.float32)
        terms.append(dot(term, mirror))
    flipped = terms[0] + (terms[1] + terms[2])
    for row in range(rel_ref.shape[0]):
        wide = jnp.broadcast_to(flipped[row : row + 1, :], (CH, TABLE))
        rolled = pltpu.roll(wide, TABLE - (CH - 1), 1, stride=1, stride_axis=0)[:, :KEYS]
        for b in range(heads):
            bias_ref[row, b] = rolled + masks[b]

    head_copies = []

    def send_heads(shift):
        for d in range(1, heads):
            copy = pltpu.make_async_remote_copy(
                src_ref=frames[shift].at[h + 1],
                dst_ref=frames[shift].at[h + 1],
                send_sem=hsend.at[shift, d - 1],
                recv_sem=hrecv.at[shift, d - 1],
                device_id={"head": lax.rem(h + d, heads)},
                device_id_type=MESH,
            )
            copy.start()
            head_copies.append(copy)

    def halo(to, source, row, side, shift):
        return pltpu.make_async_remote_copy(
            src_ref=frames[shift].at[source],
            dst_ref=frames[shift].at[row],
            send_sem=nsend.at[side, shift],
            recv_sem=nrecv.at[side, shift],
            device_id=place_of(to),
            device_id_type=MESH,
        )

    def halo_up(shift):
        return halo(half + 1, heads, 0, 0, shift)

    def halo_down(shift):
        return halo(half - 1, 1, heads + 1, 1, shift)

    has_up, has_down = half < halves - 1, half > 0

    def arrive(shift):
        for d in range(1, shards):
            piece_copies[shift * (shards - 1) + d - 1].wait_recv()
        arrived = received[shift][...]
        if cap % 16:
            arrived = arrived.astype(jnp.float32).reshape(slots, arrived.shape[2])
            return arrived.astype(jnp.bfloat16)
        return arrived.reshape(slots, arrived.shape[2])

    forward_copies = []

    def forward_weights():
        for d in range(1, heads):
            weight_copies[d - 1].wait_recv()
            source = lax.rem(h - d + heads, heads)
            copy = pltpu.make_async_remote_copy(
                src_ref=weights_ref.at[source, pl.ds(u * depth, depth)],
                dst_ref=weights_ref.at[source, pl.ds(u * depth, depth)],
                send_sem=fsend.at[d - 1],
                recv_sem=frecv.at[d - 1],
                device_id={"sub": lax.rem(u + 1, subs)},
                device_id_type=MESH,
            )
            copy.start()
            forward_copies.append(copy)

    order = None
    for shift in range(4):
        arrived = arrive(shift)
        wide = len(groups_of(shift)) * MEL
        if order is None:
            code_down = arrived[:, wide : wide + 1].astype(jnp.float32)
            code_wide = jnp.broadcast_to(code_down, (slots, slots))
            code_across = jnp.sum(jnp.where(down == across, code_wide, 0.0), axis=0, keepdims=True)
            piece = lax.broadcasted_iota(jnp.int32, (PE, slots), 0).astype(jnp.float32) + 1.0
            order = (piece == code_across).astype(jnp.float32).astype(jnp.bfloat16)
        frames[shift][h + 1] = dot(order, arrived[:, :wide]).astype(jnp.bfloat16)
        send_heads(shift)
        when(has_up & (h == heads - 1), lambda: halo_up(shift).start())
        when(has_down & (h == 0), lambda: halo_down(shift).start())
        if shift == 1:
            forward_weights()

    for copy in forward_copies + bias_copies:
        copy.wait_recv()
    loads[9].wait()

    def normed_tokens(eighth, slot):
        spread = spread_ref.at[slot]
        for shift in range(4):
            block = frames[shift][eighth].astype(jnp.float32)
            for g in groups_of(shift):
                spread[pl.ds(4 * g + shift, PE, stride=FP), :] = block[:, g * MEL : (g + 1) * MEL]
        tokens = jnp.concatenate(
            [spread[pl.ds(m, ROWS, stride=4), :] for m in range(4)], axis=1
        ).astype(jnp.bfloat16)
        summed = jnp.concatenate(
            [dot(tokens, weights_ref[g]) + sub_bias_ref[g] for g in range(heads)], axis=1
        )
        value = (summed / (1.0 + jnp.exp(-summed))).astype(jnp.bfloat16).astype(jnp.float32)
        mean = jnp.mean(value, axis=1, keepdims=True)
        centred = value - mean
        variance = jnp.mean(centred * centred, axis=1, keepdims=True)
        gain = gain_row[...].reshape(1, gain_row.shape[0])
        return (centred * lax.rsqrt(variance + EPSILON) * gain).astype(jnp.bfloat16)

    def project(eighth, normed, own):
        if own:
            rows = pl.ds(pl.multiple_of((eighth - 1) * CH, 8), CH)
            queries_ref[rows, :] = dot(normed, qkv_ref[0])[:CH] * (1.0 / math.sqrt(HDIM))
        rows = pl.ds(pl.multiple_of(eighth * CH, 8), CH)
        keys_ref[rows, :] = dot(normed, qkv_ref[1])[:CH]
        values_ref[rows, :] = dot(normed, qkv_ref[2])[:CH]

    def pass_on(shift):
        for d in range(1, heads):
            head_copies[shift * (heads - 1) + d - 1].wait_recv()
        when(has_up & (h != heads - 1), lambda: halo_up(shift).start())
        when(has_down & (h != 0), lambda: halo_down(shift).start())

    normed = normed_tokens(h + 1, 0)
    for shift in range(3):
        pass_on(shift)
    for index in range(10, 13):
        loads[index].wait()
    project(h + 1, normed, True)
    pass_on(3)
    for d in range(1, heads):
        other = lax.rem(h + d, heads) + 1
        project(other, normed_tokens(other, d), True)

    def wait_up():
        for shift in range(4):
            halo_up(shift).wait_recv()

    def wait_down():
        for shift in range(4):
            halo_down(shift).wait_recv()

    when(u == 0, wait_down)
    when(u != 0, wait_up)
    near = jnp.where(u == 0, heads + 1, 0)
    project(near, normed_tokens(near, heads), False)
    when((u == 0) & has_down, wait_up)
    when((u != 0) & has_up, wait_down)
    far = jnp.where(u == 0, 0, heads + 1)
    project(far, normed_tokens(far, heads + 1), False)

    for copy in bias_copies + weight_copies + piece_copies + head_copies + forward_copies:
        copy.wait_send()
    for shift in range(4):
        when(has_up, lambda: halo_up(shift).wait_send())
        when(has_down, lambda: halo_down(shift).wait_send())


def back_kernel(queries, keys, values, bias_ref, context_out, context_ref, sem):
    blocks = bias_ref.shape[1]
    width = queries.shape[1]
    span = 3 * CH
    lane = lax.broadcasted_iota(jnp.int32, (1, LANES), 1)
    blank = jnp.zeros((KEYS - span, LANES), jnp.float32)
    ones = jnp.ones((KEYS, LANES), jnp.bfloat16)
    copies = []
    for pair in range(width // LANES):
        lanes = slice(pair * LANES, (pair + 1) * LANES)
        for b in range(blocks):
            query = queries[b * CH : (b + 1) * CH, lanes].astype(jnp.bfloat16).astype(jnp.float32)
            key = jnp.concatenate([keys[b * CH : b * CH + span, lanes], blank], axis=0)
            value = jnp.concatenate([values[b * CH : b * CH + span, lanes], blank], axis=0)
            both = jnp.concatenate(
                [jnp.where(lane < HDIM, query, 0.0), jnp.where(lane < HDIM, 0.0, query)], axis=0
            ).astype(jnp.bfloat16)
            scores = lax.dot_general(
                both, key.astype(jnp.bfloat16), (((1,), (1,)), ((), ())),
                preferred_element_type=jnp.float32,
            )
            shift = jnp.concatenate([bias_ref[2 * pair, b], bias_ref[2 * pair + 1, b]], axis=0)
            scores = scores + shift
            raised = jnp.exp(scores - jnp.max(scores, axis=1, keepdims=True)).astype(jnp.bfloat16)
            out = dot(raised, jnp.concatenate([value.astype(jnp.bfloat16), ones], axis=1))
            out = jnp.where(
                jnp.concatenate([lane, lane], axis=1) % LANES < HDIM, out[:CH], out[CH:]
            )
            joined = out[:, :LANES] / out[:, LANES:]
            context_ref[b * CH : (b + 1) * CH, lanes] = joined.astype(jnp.bfloat16)
        copy = pltpu.make_async_copy(
            context_ref.at[:, lanes], context_out.at[:, lanes], sem.at[pair]
        )
        copy.start()
        copies.append(copy)
    for copy in copies:
        copy.wait()


def local(
    shards, heads, subs,
    wave_pieces, piece_target, utt_lengths, sub_weight, sub_bias, norm_gain, qkv_weight, rel_bias,
):
    slots, samples = wave_pieces.shape[3:]
    cap = slots // shards
    depth, width = sub_weight.shape
    whole_width = qkv_weight.shape[0]
    vmem = pl.BlockSpec(memory_space=pltpu.VMEM)
    sizes = [len(groups_of(shift)) * MEL for shift in range(4)]
    payloads = [size + (shift == 0) * MEL for shift, size in enumerate(sizes)]
    dma = pltpu.SemaphoreType.DMA
    hbm = pl.BlockSpec(memory_space=pltpu.HBM)
    heads_here = rel_bias.shape[0]
    tokens_here = heads * CH
    queries, keys, values, position_bias = pl.pallas_call(
        functools.partial(front_kernel, shards, heads, subs),
        out_shape=(
            jax.ShapeDtypeStruct((tokens_here, width), jnp.float32),
            jax.ShapeDtypeStruct((tokens_here + 2 * CH, width), jnp.float32),
            jax.ShapeDtypeStruct((tokens_here + 2 * CH, width), jnp.float32),
            jax.ShapeDtypeStruct((heads_here, heads, CH, KEYS), jnp.float32),
        ),
        in_specs=[hbm] * 11,
        out_specs=(vmem,) * 4,
        scratch_shapes=[
            pltpu.VMEM((slots, samples), jnp.float32),
            pltpu.VMEM((1, slots), jnp.int32),
            pltpu.VMEM((1, NFFT), jnp.float32),
            pltpu.VMEM((2, 3 * NFFT // 2, NFFT // 2), jnp.bfloat16),
            pltpu.VMEM((NFFT, MEL), jnp.bfloat16),
            pltpu.VMEM((width,), jnp.bfloat16),
            pltpu.VMEM((whole_width,), jnp.float32),
            pltpu.VMEM(rel_bias.shape, jnp.float32),
            pltpu.VMEM((heads, depth, width), jnp.bfloat16),
            pltpu.VMEM((heads, 1, width), jnp.float32),
            pltpu.VMEM((3, whole_width, width), jnp.bfloat16),
            pltpu.SMEM(utt_lengths.shape, jnp.int32),
            pltpu.VMEM((heads + 2, 4 * ROWS, MEL), jnp.float32),
            *[pltpu.VMEM((shards, cap, wide), jnp.bfloat16) for wide in payloads],
            *[pltpu.VMEM((shards, cap, wide), jnp.bfloat16) for wide in payloads],
            *[pltpu.VMEM((heads + 2, PE, wide), jnp.bfloat16) for wide in sizes],
            dma((13,)),
            dma((heads - 1,)), dma((heads - 1,)), dma((heads - 1,)), dma((heads - 1,)),
            dma((4, shards - 1)), dma((4, shards - 1)),
            dma((4, heads - 1)), dma((4, heads - 1)),
            dma((2, 4)), dma((2, 4)), dma((heads - 1,)), dma((heads - 1,)),
        ],
        compiler_params=pltpu.CompilerParams(
            collective_id=0, has_side_effects=True, vmem_limit_bytes=36 << 20
        ),
        name="front",
    )(
        *[
            pltpu.with_memory_space_constraint(value, pltpu.HBM)
            for value in (
                wave_pieces.reshape(slots, samples),
                piece_target.reshape(1, slots),
                sub_weight,
                jnp.asarray(window_table()),
                jnp.asarray(fourier_tables()),
                jnp.asarray(mel_table()),
                sub_bias,
                norm_gain,
                rel_bias,
                jnp.transpose(qkv_weight, (1, 0, 2)),
                utt_lengths,
            )
        ]
    )

    return pl.pallas_call(
        back_kernel,
        out_shape=jax.ShapeDtypeStruct((tokens_here, width), jnp.bfloat16),
        in_specs=[vmem] * 4,
        out_specs=hbm,
        scratch_shapes=[
            pltpu.VMEM((tokens_here, width), jnp.bfloat16),
            dma((width // LANES,)),
        ],
        compiler_params=pltpu.CompilerParams(vmem_limit_bytes=24 << 20),
        name="back",
    )(queries, keys, values, position_bias)


def solution(mesh):
    placed = (
        P(("groups", "seq"), "head", "sub", None, None),
        P(("groups", "seq"), "head", "sub", None),
        P("groups"),
        P(None, "head"),
        P("head"),
        P(),
        P(None, None, "head"),
        P("head", None),
    )
    return jax.shard_map(
        functools.partial(local, mesh.shape["seq"], mesh.shape["head"], mesh.shape["sub"]),
        mesh=mesh,
        in_specs=placed,
        out_specs=P(("groups", "seq", "sub"), "head"),
        check_vma=False,
    )
```

```python
import functools
import math

import jax
import jax.numpy as jnp
import numpy as np
from jax import lax
from jax.experimental import pallas as pl
from jax.experimental.pallas import tpu as pltpu
from jax.sharding import PartitionSpec as P

HDIM = 64
MEL = 128
NFFT = 512
HOP = 160
FP = 17
CH = 136
PE = 32
LANES = 128
TABLE = 640
KEYS = 512
ROWS = 144


SAMPLE_RATE = 16000.0
EPSILON = 1e-05
MASKED = -1e30
MESH = pl.DeviceIdType.MESH


def split_bf16(table):
    high = table.astype(np.float32).astype(jnp.bfloat16)
    low = (table - high.astype(np.float64)).astype(np.float32).astype(jnp.bfloat16)
    return np.stack([high, low])


def stacked(table):
    high, low = split_bf16(table)
    return np.concatenate([high, high, low], axis=0)


def window_table():
    return (0.5 - 0.5 * np.cos(2.0 * np.pi / NFFT * np.arange(NFFT)))[None].astype(np.float32)


def fourier_tables():
    half = NFFT // 2
    sample = np.arange(half)[:, None]

    def phase(bins):
        return (sample * bins[None, :] % NFFT) * (2.0 * np.pi / NFFT)

    even, odd = np.arange(0, half, 2), np.arange(1, half, 2)
    even_sine = np.sin(phase(even))
    even_sine[:, 0] = np.cos(phase(np.array([half])))[:, 0]
    even_table = np.concatenate([np.cos(phase(even)), even_sine], axis=1)
    odd_table = np.concatenate([np.cos(phase(odd)), np.sin(phase(odd))], axis=1)
    return np.stack([stacked(even_table), stacked(odd_table)])


def mel_table():
    bin_total = NFFT // 2 + 1
    highest = 2595.0 * math.log10(1.0 + SAMPLE_RATE / 2.0 / 700.0)
    points = np.arange(MEL + 2) * (highest / (MEL + 1))
    hertz = 700.0 * (np.power(10.0, points / 2595.0) - 1.0)
    centres = np.arange(bin_total) * (SAMPLE_RATE / NFFT)
    rising = (centres[:, None] - hertz[None, :-2]) / (hertz[1:-1] - hertz[:-2])[None, :]
    falling = (hertz[None, 2:] - centres[:, None]) / (hertz[2:] - hertz[1:-1])[None, :]
    table = np.maximum(0.0, np.minimum(rising, falling))
    sine_even = table[0 : bin_total - 1 : 2].copy()
    sine_even[0] = table[bin_total - 1]
    rows = np.concatenate(
        [table[0 : bin_total - 1 : 2], sine_even, table[1::2], table[1::2]], axis=0
    )
    return rows.astype(np.float32).astype(jnp.bfloat16)


def dot(left, right):
    return jnp.dot(left, right, preferred_element_type=jnp.float32)


def dot_split(value, table):
    value_high = value.astype(jnp.bfloat16)
    value_low = (value - value_high.astype(jnp.float32)).astype(jnp.bfloat16)
    return dot(jnp.concatenate([value_high, value_low, value_high], axis=1), table)


PHASES = (
    (0, (0, 1)),
    (0, (2, 3, 4)),
    (1, (0, 1, 2, 3)),
    (2, (0, 1, 2, 3)),
    (3, (0, 1, 2, 3)),
)
COUNT = len(PHASES)
WEIGHT_CHUNKS = 2


def flipped_bits(index, bits):
    for k in range(bits.bit_length()):
        if bits >> k & 1:
            index = index + (1 - 2 * (index // (1 << k) % 2)) * (1 << k)
    return index


def front_kernel(
    groups, shards, heads, subs,
    wave_in, target_in, weight_ref, window_in, fourier_in, mel_in, sub_bias_in, gain_in, rel_in,
    qkv_in, lengths_in,
    queries_ref, keys_ref, values_ref, bias_ref,
    wave_ref, target_ref, window_ref, fourier_ref, mel_ref, sub_bias_row, gain_row, rel_ref,
    weights_ref, sub_bias_ref, qkv_ref, lengths_ref, spread_ref,
    *rest,
):
    packed, received, frames = rest[:COUNT], rest[COUNT : 2 * COUNT], rest[2 * COUNT : 3 * COUNT]
    (
        lsem, wsend, wrecv, ysend, yrecv, fsend, frecv, asend, arecv, hsend, hrecv, nsend, nrecv,
        bsend, brecv, ksend, krecv,
    ) = rest[3 * COUNT :]
    mine = lax.axis_index("groups")
    s, h, u = lax.axis_index("seq"), lax.axis_index("head"), lax.axis_index("sub")
    half = s * subs + u
    halves = shards * subs
    slots = wave_ref.shape[0]
    cap = slots // shards
    depth = weight_ref.shape[0] // (subs * groups * WEIGHT_CHUNKS)

    def place_of(index):
        return {"seq": index // subs, "sub": index % subs}

    def when(condition, action):
        @pl.when(condition)
        def _():
            action()

    pairs = (
        (target_in, target_ref), (wave_in, wave_ref), (window_in, window_ref),
        (fourier_in, fourier_ref), (mel_in, mel_ref), (sub_bias_in, sub_bias_row),
        (gain_in, gain_row), (rel_in, rel_ref), (lengths_in, lengths_ref),
        (weight_ref, weights_ref.at[h]),
        (qkv_in.at[0], qkv_ref.at[0]), (qkv_in.at[1], qkv_ref.at[1]),
        (qkv_in.at[2], qkv_ref.at[2]),
    )
    loads = [pltpu.make_async_copy(a, b, lsem.at[i]) for i, (a, b) in enumerate(pairs)]
    for load in loads[:9]:
        load.start()

    barrier = pltpu.get_barrier_semaphore()
    for d in range(1, shards):
        pl.semaphore_signal(
            barrier, inc=1, device_id={"seq": lax.rem(s + d, shards)}, device_id_type=MESH
        )
    for d in range(1, heads):
        pl.semaphore_signal(
            barrier, inc=1, device_id={"head": lax.rem(h + d, heads)}, device_id_type=MESH
        )

    for d in range(1, groups):
        pl.semaphore_signal(
            barrier, inc=1, device_id={"groups": lax.rem(mine + d, groups)}, device_id_type=MESH
        )

    @pl.when(half > 0)
    def _():
        pl.semaphore_signal(barrier, inc=1, device_id=place_of(half - 1), device_id_type=MESH)

    @pl.when(half < halves - 1)
    def _():
        pl.semaphore_signal(barrier, inc=1, device_id=place_of(half + 1), device_id_type=MESH)

    inner = jnp.where(half > 0, 1, 0) + jnp.where(half < halves - 1, 1, 0)
    pl.semaphore_wait(barrier, shards - 1 + heads - 1 + groups - 1 + inner)

    sibling = {"sub": lax.rem(u + 1, subs)}

    def weight_rows(group, chunk):
        return pl.ds(((u * groups + group) * WEIGHT_CHUNKS + chunk) * depth, depth)

    def send_weights(source, owner, group, chunk, send_sem, recv_sem, device):
        rows = weight_rows(group, chunk)
        copy = pltpu.make_async_remote_copy(
            src_ref=source.at[rows],
            dst_ref=weights_ref.at[owner, rows],
            send_sem=send_sem,
            recv_sem=recv_sem,
            device_id=device,
            device_id_type=MESH,
        )
        copy.start()
        return copy

    weight_copies, bias_copies = [], []
    for chunk in range(WEIGHT_CHUNKS):
        for d in range(1, heads):
            weight_copies.append(
                send_weights(
                    weight_ref, h, mine, chunk, wsend.at[chunk, d - 1], wrecv.at[chunk, d - 1],
                    {"head": lax.rem(h + d, heads)},
                )
            )

    loads[0].wait()
    target = target_ref[...]
    owner = jnp.where(target >= 0, lax.shift_right_arithmetic(target, 5), shards)
    place = jnp.bitwise_and(target, PE - 1)
    down = lax.broadcasted_iota(jnp.int32, (slots, slots), 0)
    across = lax.broadcasted_iota(jnp.int32, (slots, slots), 1)
    owner_wide = jnp.broadcast_to(owner, (slots, slots))
    owner_down = jnp.sum(jnp.where(down == across, owner_wide, 0), axis=1, keepdims=True)
    rank = jnp.sum(
        jnp.where((owner_down == owner_wide) & (down < across), 1, 0), axis=0, keepdims=True
    )
    goal = jnp.where(owner < shards, owner * cap + rank, -1)
    chosen = down == goal
    select = chosen.astype(jnp.float32).astype(jnp.bfloat16)
    code = jnp.sum(jnp.where(chosen, place + 1, 0), axis=1, keepdims=True).astype(jnp.float32)
    code = jnp.broadcast_to(code, (slots, LANES)).astype(jnp.bfloat16)

    piece_copies = []
    for index in range(1, 5):
        loads[index].wait()
    for load in loads[9:]:
        load.start()
    for phase, (shift, frame_groups) in enumerate(PHASES):
        wave = wave_ref[...]
        if shift:
            wave = pltpu.roll(wave, wave.shape[1] - 32 * shift, 1)
        pieces = [
            wave[:, LANES * (5 * g + shift) : LANES * (5 * g + shift) + NFFT] * window_ref[...]
            for g in frame_groups
        ]
        pieces = jnp.concatenate(pieces, axis=0)
        low, high = pieces[:, : NFFT // 2], pieces[:, NFFT // 2 :]
        even = dot_split(low + high, fourier_ref[0])
        odd = dot_split(low - high, fourier_ref[1])
        squares = jnp.concatenate([even * even, odd * odd], axis=1).astype(jnp.bfloat16)
        energy = dot(squares, mel_ref[...])
        logs = jnp.log(1.0 + energy).astype(jnp.bfloat16)
        count = len(frame_groups)
        logs = jnp.concatenate([logs[n * slots : (n + 1) * slots] for n in range(count)], axis=1)
        rows = dot(select, logs).astype(jnp.bfloat16)
        for t in range(shards):
            packed[phase][t, :, : count * MEL] = rows[t * cap : (t + 1) * cap]
            if phase == 0:
                packed[0][t, :, count * MEL :] = code[t * cap : (t + 1) * cap]
        for d in range(shards - 1, 0, -1):
            to = flipped_bits(s, d)
            copy = pltpu.make_async_remote_copy(
                src_ref=packed[phase].at[to],
                dst_ref=received[phase].at[s],
                send_sem=asend.at[phase, d - 1],
                recv_sem=arecv.at[phase, d - 1],
                device_id={"seq": to},
                device_id_type=MESH,
            )
            copy.start()
            piece_copies.append(copy)
        received[phase][s] = packed[phase][s]

    loads[5].wait()
    sub_bias_ref[h] = sub_bias_row[...].astype(jnp.float32).reshape(1, sub_bias_row.shape[0])
    for d in range(1, heads):
        copy = pltpu.make_async_remote_copy(
            src_ref=sub_bias_ref.at[h],
            dst_ref=sub_bias_ref.at[h],
            send_sem=bsend.at[d - 1],
            recv_sem=brecv.at[d - 1],
            device_id={"head": lax.rem(h + d, heads)},
            device_id_type=MESH,
        )
        copy.start()
        bias_copies.append(copy)

    @pl.when(half == 0)
    def _():
        for phase in range(COUNT):
            frames[phase][0] = jnp.zeros(frames[phase].shape[1:], jnp.bfloat16)

    @pl.when(half == halves - 1)
    def _():
        for phase in range(COUNT):
            frames[phase][heads + 1] = jnp.zeros(frames[phase].shape[1:], jnp.bfloat16)

    for slot in range(spread_ref.shape[0]):
        spread_ref[slot, PE * FP :] = jnp.zeros((4 * ROWS - PE * FP, MEL), jnp.float32)

    blank_rows = keys_ref.shape[0] - (heads + 2) * ROWS
    for out in (keys_ref, values_ref):
        out[(heads + 2) * ROWS :, :] = jnp.zeros((blank_rows, out.shape[1]), jnp.bfloat16)

    loads[6].wait()
    loads[7].wait()
    loads[8].wait()
    first_token, token_total = half * heads * CH, halves * heads * CH
    masks = []
    for b in range(heads):
        query_pos = first_token + b * CH + lax.broadcasted_iota(jnp.int32, (CH, 1), 0)
        key_index = lax.broadcasted_iota(jnp.int32, (1, KEYS), 1)
        gap = jnp.zeros_like(key_index)
        for e in range(1, 4):
            gap = gap + (key_index >= e * ROWS).astype(jnp.int32)
        key_in = key_index - gap * ROWS
        key_pos = first_token + (b - 1 + gap) * CH + key_in
        end = jnp.int32(0)
        query_utt = jnp.zeros_like(query_pos)
        key_utt = jnp.zeros_like(key_pos)
        for r in range(lengths_ref.shape[0]):
            end = end + lengths_ref[r]
            query_utt = query_utt + (query_pos >= end).astype(jnp.int32)
            key_utt = key_utt + (key_pos >= end).astype(jnp.int32)
        inside = (key_pos >= 0) & (key_pos < token_total) & (gap < 3) & (key_in < CH)
        key_utt = jnp.where(inside, key_utt, -1)
        masks.append(jnp.where(query_utt == key_utt, 0.0, MASKED))
    taps = rel_ref.shape[1]
    mirror = lax.broadcasted_iota(jnp.int32, (taps, TABLE), 0) + lax.broadcasted_iota(
        jnp.int32, (taps, TABLE), 1
    )
    mirror = (mirror == taps - 1).astype(jnp.float32).astype(jnp.bfloat16)
    rest = rel_ref[...]
    terms = []
    for _ in range(3):
        term = rest.astype(jnp.bfloat16)
        rest = rest - term.astype(jnp.float32)
        terms.append(dot(term, mirror))
    key_lane = lax.broadcasted_iota(jnp.int32, (1, KEYS), 1)
    flipped = terms[0] + (terms[1] + terms[2])
    for row in range(rel_ref.shape[0]):
        wide = jnp.broadcast_to(flipped[row : row + 1, :], (CH, TABLE))
        wide = pltpu.roll(wide, TABLE - (CH - 1), 1, stride=1, stride_axis=0)
        once = pltpu.roll(wide, ROWS - CH, 1)[:, :KEYS]
        twice = pltpu.roll(wide, 2 * (ROWS - CH), 1)[:, :KEYS]
        spaced = jnp.where(
            key_lane < ROWS, wide[:, :KEYS], jnp.where(key_lane < 2 * ROWS, once, twice)
        )
        for b in range(heads):
            bias_ref[row, b] = spaced + masks[b]

    head_copies = []

    def send_heads(phase):
        for d in range(1, heads):
            copy = pltpu.make_async_remote_copy(
                src_ref=frames[phase].at[h + 1],
                dst_ref=frames[phase].at[h + 1],
                send_sem=hsend.at[phase, d - 1],
                recv_sem=hrecv.at[phase, d - 1],
                device_id={"head": lax.rem(h + d, heads)},
                device_id_type=MESH,
            )
            copy.start()
            head_copies.append(copy)

    def halo(to, source, row, side, phase):
        return pltpu.make_async_remote_copy(
            src_ref=frames[phase].at[source],
            dst_ref=frames[phase].at[row],
            send_sem=nsend.at[phase],
            recv_sem=nrecv.at[phase],
            device_id=place_of(to),
            device_id_type=MESH,
        )

    def halo_up(phase):
        return halo(half + 1, heads, 0, 0, phase)

    def halo_down(phase):
        return halo(half - 1, 1, heads + 1, 1, phase)

    has_up, has_down = (u != 0) & (half < halves - 1), (u == 0) & (half > 0)

    def arrive(phase):
        for d in range(1, shards):
            piece_copies[phase * (shards - 1) + d - 1].wait_recv()
        arrived = received[phase][...]
        if cap % 16:
            arrived = arrived.astype(jnp.float32).reshape(slots, arrived.shape[2])
            return arrived.astype(jnp.bfloat16)
        return arrived.reshape(slots, arrived.shape[2])

    across_copies, forward_copies = [], []

    def forward(source, group, chunk, d, index):
        forward_copies.append(
            send_weights(
                weights_ref.at[source], source, group, chunk,
                fsend.at[chunk, d - 1, index], frecv.at[chunk, d - 1, index], sibling,
            )
        )

    def spread_weights():
        for chunk in range(WEIGHT_CHUNKS):
            for d in range(1, heads):
                source = lax.rem(h - d + heads, heads)
                weight_copies[chunk * (heads - 1) + d - 1].wait_recv()
                for e in range(1, groups):
                    across_copies.append(
                        send_weights(
                            weights_ref.at[source], source, mine, chunk,
                            ysend.at[chunk, d - 1, e - 1], yrecv.at[chunk, d - 1, e - 1],
                            {"groups": lax.rem(mine + e, groups)},
                        )
                    )
                forward(source, mine, chunk, d, 0)

    def forward_weights():
        index = 0
        for chunk in range(WEIGHT_CHUNKS):
            for d in range(1, heads):
                source = lax.rem(h - d + heads, heads)
                for e in range(1, groups):
                    across_copies[index].wait_recv()
                    index += 1
                    forward(source, lax.rem(mine - e + groups, groups), chunk, d, e)

    spread_weights()
    order = None
    for phase, (shift, frame_groups) in enumerate(PHASES):
        if phase == COUNT - 1:
            forward_weights()
        arrived = arrive(phase)
        wide = len(frame_groups) * MEL
        if order is None:
            code_down = arrived[:, wide : wide + 1].astype(jnp.float32)
            code_wide = jnp.broadcast_to(code_down, (slots, slots))
            code_across = jnp.sum(jnp.where(down == across, code_wide, 0.0), axis=0, keepdims=True)
            piece = lax.broadcasted_iota(jnp.int32, (PE, slots), 0).astype(jnp.float32) + 1.0
            order = (piece == code_across).astype(jnp.float32).astype(jnp.bfloat16)
        frames[phase][h + 1] = dot(order, arrived[:, :wide]).astype(jnp.bfloat16)
        send_heads(phase)
        when(has_up & (h == heads - 1), lambda: halo_up(phase).start())
        when(has_down & (h == 0), lambda: halo_down(phase).start())

    for copy in forward_copies + bias_copies:
        copy.wait_recv()
    loads[9].wait()

    def normed_tokens(eighth, slot):
        spread = spread_ref.at[slot]
        for phase, (shift, frame_groups) in enumerate(PHASES):
            block = frames[phase][eighth].astype(jnp.float32)
            for n, g in enumerate(frame_groups):
                spread[pl.ds(4 * g + shift, PE, stride=FP), :] = block[:, n * MEL : (n + 1) * MEL]
        tokens = jnp.concatenate(
            [spread[pl.ds(m, ROWS, stride=4), :] for m in range(4)], axis=1
        ).astype(jnp.bfloat16)
        summed = jnp.concatenate(
            [dot(tokens, weights_ref[g]) + sub_bias_ref[g] for g in range(heads)], axis=1
        )
        value = (summed / (1.0 + jnp.exp(-summed))).astype(jnp.bfloat16).astype(jnp.float32)
        mean = jnp.mean(value, axis=1, keepdims=True)
        centred = value - mean
        variance = jnp.mean(centred * centred, axis=1, keepdims=True)
        gain = gain_row[...].reshape(1, gain_row.shape[0])
        return (centred * lax.rsqrt(variance + EPSILON) * gain).astype(jnp.bfloat16)

    def project(eighth, normed, own):
        if own:
            rows = pl.ds(pl.multiple_of((eighth - 1) * CH, 8), CH)
            queries_ref[rows, :] = dot(normed, qkv_ref[0])[:CH] * (1.0 / math.sqrt(HDIM))
        rows = pl.ds(pl.multiple_of(eighth * ROWS, ROWS), ROWS)
        keys_ref[rows, :] = dot(normed, qkv_ref[1]).astype(jnp.bfloat16)
        values_ref[rows, :] = dot(normed, qkv_ref[2]).astype(jnp.bfloat16)

    def pass_on(phase):
        for d in range(1, heads):
            head_copies[phase * (heads - 1) + d - 1].wait_recv()
        when(has_up & (h != heads - 1), lambda: halo_up(phase).start())
        when(has_down & (h != 0), lambda: halo_down(phase).start())

    normed = normed_tokens(h + 1, 0)
    for phase in range(COUNT - 1):
        pass_on(phase)
    for index in range(10, 13):
        loads[index].wait()
    project(h + 1, normed, True)
    pass_on(COUNT - 1)
    for d in range(1, heads):
        other = lax.rem(h + d, heads) + 1
        project(other, normed_tokens(other, d), True)

    edge = pl.ds(pl.multiple_of(jnp.where(u == 0, heads, 1) * ROWS, ROWS), ROWS)
    landing = pl.ds(pl.multiple_of(jnp.where(u == 0, 0, heads + 1) * ROWS, ROWS), ROWS)
    edge_copies = []
    for index, out in enumerate((keys_ref, values_ref)):
        copy = pltpu.make_async_remote_copy(
            src_ref=out.at[edge],
            dst_ref=out.at[landing],
            send_sem=ksend.at[index],
            recv_sem=krecv.at[index],
            device_id=sibling,
            device_id_type=MESH,
        )
        copy.start()
        edge_copies.append(copy)

    def wait_up():
        for phase in range(COUNT):
            halo_up(phase).wait_recv()

    def wait_down():
        for phase in range(COUNT):
            halo_down(phase).wait_recv()

    when(has_down, wait_up)
    when(has_up, wait_down)
    far = jnp.where(u == 0, 0, heads + 1)
    project(far, normed_tokens(far, heads), False)

    for copy in edge_copies:
        copy.wait()
    for copy in (
        bias_copies + weight_copies + across_copies + forward_copies + piece_copies + head_copies
    ):
        copy.wait_send()
    for phase in range(COUNT):
        when(has_up, lambda: halo_up(phase).wait_send())
        when(has_down, lambda: halo_down(phase).wait_send())


def back_kernel(queries, keys, values, bias_ref, context_out, context_ref, sem):
    blocks = bias_ref.shape[1]
    width = queries.shape[1]
    lane = lax.broadcasted_iota(jnp.int32, (1, LANES), 1)
    ones = jnp.ones((KEYS, LANES), jnp.bfloat16)
    copies = []
    for pair in range(width // LANES):
        lanes = slice(pair * LANES, (pair + 1) * LANES)
        for b in range(blocks):
            query = queries[b * CH : (b + 1) * CH, lanes]
            key = keys[b * ROWS : b * ROWS + KEYS, lanes]
            value = values[b * ROWS : b * ROWS + KEYS, lanes]
            both = jnp.concatenate(
                [jnp.where(lane < HDIM, query, 0.0), jnp.where(lane < HDIM, 0.0, query)], axis=0
            ).astype(jnp.bfloat16)
            scores = lax.dot_general(
                both, key, (((1,), (1,)), ((), ())), preferred_element_type=jnp.float32
            )
            shift = jnp.concatenate([bias_ref[2 * pair, b], bias_ref[2 * pair + 1, b]], axis=0)
            scores = scores + shift
            raised = jnp.exp(scores - jnp.max(scores, axis=1, keepdims=True)).astype(jnp.bfloat16)
            out = dot(raised, jnp.concatenate([value, ones], axis=1))
            out = jnp.where(
                jnp.concatenate([lane, lane], axis=1) % LANES < HDIM, out[:CH], out[CH:]
            )
            joined = out[:, :LANES] / out[:, LANES:]
            context_ref[b * CH : (b + 1) * CH, lanes] = joined.astype(jnp.bfloat16)
        copy = pltpu.make_async_copy(
            context_ref.at[:, lanes], context_out.at[:, lanes], sem.at[pair]
        )
        copy.start()
        copies.append(copy)
    for copy in copies:
        copy.wait()


def local(
    groups, shards, heads, subs,
    wave_pieces, piece_target, utt_lengths, sub_weight, sub_bias, norm_gain, qkv_weight, rel_bias,
):
    slots, samples = wave_pieces.shape[3:]
    cap = slots // shards
    depth, width = sub_weight.shape
    whole_width = qkv_weight.shape[0]
    vmem = pl.BlockSpec(memory_space=pltpu.VMEM)
    sizes = [len(frame_groups) * MEL for _, frame_groups in PHASES]
    payloads = [size + (phase == 0) * MEL for phase, size in enumerate(sizes)]
    dma = pltpu.SemaphoreType.DMA
    hbm = pl.BlockSpec(memory_space=pltpu.HBM)
    heads_here = rel_bias.shape[0]
    tokens_here = heads * CH
    key_rows = (heads - 1) * ROWS + KEYS
    others, parts = heads - 1, WEIGHT_CHUNKS
    queries, keys, values, position_bias = pl.pallas_call(
        functools.partial(front_kernel, groups, shards, heads, subs),
        out_shape=(
            jax.ShapeDtypeStruct((tokens_here, width), jnp.float32),
            jax.ShapeDtypeStruct((key_rows, width), jnp.bfloat16),
            jax.ShapeDtypeStruct((key_rows, width), jnp.bfloat16),
            jax.ShapeDtypeStruct((heads_here, heads, CH, KEYS), jnp.float32),
        ),
        in_specs=[hbm] * 11,
        out_specs=(vmem,) * 4,
        scratch_shapes=[
            pltpu.VMEM((slots, samples), jnp.float32),
            pltpu.VMEM((1, slots), jnp.int32),
            pltpu.VMEM((1, NFFT), jnp.float32),
            pltpu.VMEM((2, 3 * NFFT // 2, NFFT // 2), jnp.bfloat16),
            pltpu.VMEM((NFFT, MEL), jnp.bfloat16),
            pltpu.VMEM((width,), jnp.bfloat16),
            pltpu.VMEM((whole_width,), jnp.float32),
            pltpu.VMEM(rel_bias.shape, jnp.float32),
            pltpu.VMEM((heads, depth, width), jnp.bfloat16),
            pltpu.VMEM((heads, 1, width), jnp.float32),
            pltpu.VMEM((3, whole_width, width), jnp.bfloat16),
            pltpu.SMEM(utt_lengths.shape, jnp.int32),
            pltpu.VMEM((heads + 2, 4 * ROWS, MEL), jnp.float32),
            *[pltpu.VMEM((shards, cap, wide), jnp.bfloat16) for wide in payloads],
            *[pltpu.VMEM((shards, cap, wide), jnp.bfloat16) for wide in payloads],
            *[pltpu.VMEM((heads + 2, PE, wide), jnp.bfloat16) for wide in sizes],
            dma((13,)),
            dma((parts, others)), dma((parts, others)),
            dma((parts, others, groups - 1)), dma((parts, others, groups - 1)),
            dma((parts, others, groups)), dma((parts, others, groups)),
            dma((COUNT, shards - 1)), dma((COUNT, shards - 1)),
            dma((COUNT, others)), dma((COUNT, others)),
            dma((COUNT,)), dma((COUNT,)), dma((others,)), dma((others,)), dma((2,)), dma((2,)),
        ],
        compiler_params=pltpu.CompilerParams(
            collective_id=0, has_side_effects=True, vmem_limit_bytes=36 << 20
        ),
        name="front",
    )(
        *[
            pltpu.with_memory_space_constraint(value, pltpu.HBM)
            for value in (
                wave_pieces.reshape(slots, samples),
                piece_target.reshape(1, slots),
                sub_weight,
                jnp.asarray(window_table()),
                jnp.asarray(fourier_tables()),
                jnp.asarray(mel_table()),
                sub_bias,
                norm_gain,
                rel_bias,
                jnp.transpose(qkv_weight, (1, 0, 2)),
                utt_lengths,
            )
        ]
    )

    return pl.pallas_call(
        back_kernel,
        out_shape=jax.ShapeDtypeStruct((tokens_here, width), jnp.bfloat16),
        in_specs=[vmem] * 4,
        out_specs=hbm,
        scratch_shapes=[
            pltpu.VMEM((tokens_here, width), jnp.bfloat16),
            dma((width // LANES,)),
        ],
        compiler_params=pltpu.CompilerParams(vmem_limit_bytes=24 << 20),
        name="back",
    )(queries, keys, values, position_bias)


def solution(mesh):
    placed = (
        P(("groups", "seq"), "head", "sub", None, None),
        P(("groups", "seq"), "head", "sub", None),
        P("groups"),
        P(None, "head"),
        P("head"),
        P(),
        P(None, None, "head"),
        P("head", None),
    )
    return jax.shard_map(
        functools.partial(
            local, mesh.shape["groups"], mesh.shape["seq"], mesh.shape["head"], mesh.shape["sub"]
        ),
        mesh=mesh,
        in_specs=placed,
        out_specs=P(("groups", "seq", "sub"), "head"),
        check_vma=False,
    )
```

```python
import functools
import math

import jax
import jax.numpy as jnp
import numpy as np
from jax import lax
from jax.experimental import pallas as pl
from jax.experimental.pallas import tpu as pltpu
from jax.sharding import PartitionSpec as P

HDIM = 64
MEL = 128
NFFT = 512
HOP = 160
FP = 17
CH = 136
PE = 32
LANES = 128
TABLE = 640
KEYS = 512
ROWS = 144


SAMPLE_RATE = 16000.0
EPSILON = 1e-05
MASKED = -1e30
MESH = pl.DeviceIdType.MESH


def split_bf16(table):
    high = table.astype(np.float32).astype(jnp.bfloat16)
    low = (table - high.astype(np.float64)).astype(np.float32).astype(jnp.bfloat16)
    return np.stack([high, low])


def window_table():
    return (0.5 - 0.5 * np.cos(2.0 * np.pi / NFFT * np.arange(NFFT)))[None].astype(np.float32)


def fourier_tables():
    half = NFFT // 2
    sample = np.arange(half)[:, None]

    def phase(bins):
        return (sample * bins[None, :] % NFFT) * (2.0 * np.pi / NFFT)

    even, odd = np.arange(0, half, 2), np.arange(1, half, 2)
    even_sine = np.sin(phase(even))
    even_sine[:, 0] = np.cos(phase(np.array([half])))[:, 0]
    even_table = np.concatenate([np.cos(phase(even)), even_sine], axis=1)
    odd_table = np.concatenate([np.cos(phase(odd)), np.sin(phase(odd))], axis=1)
    return np.stack([np.concatenate(split_bf16(t), axis=0) for t in (even_table, odd_table)])


def mel_table():
    bin_total = NFFT // 2 + 1
    highest = 2595.0 * math.log10(1.0 + SAMPLE_RATE / 2.0 / 700.0)
    points = np.arange(MEL + 2) * (highest / (MEL + 1))
    hertz = 700.0 * (np.power(10.0, points / 2595.0) - 1.0)
    centres = np.arange(bin_total) * (SAMPLE_RATE / NFFT)
    rising = (centres[:, None] - hertz[None, :-2]) / (hertz[1:-1] - hertz[:-2])[None, :]
    falling = (hertz[None, 2:] - centres[:, None]) / (hertz[2:] - hertz[1:-1])[None, :]
    table = np.maximum(0.0, np.minimum(rising, falling))
    sine_even = table[0 : bin_total - 1 : 2].copy()
    sine_even[0] = table[bin_total - 1]
    rows = np.concatenate(
        [table[0 : bin_total - 1 : 2], sine_even, table[1::2], table[1::2]], axis=0
    )
    return rows.astype(np.float32).astype(jnp.bfloat16)


def dot(left, right):
    return jnp.dot(left, right, preferred_element_type=jnp.float32)


def dot_split(value, table):
    value_high = value.astype(jnp.bfloat16)
    value_low = (value - value_high.astype(jnp.float32)).astype(jnp.bfloat16)
    depth = value.shape[1]
    table = jnp.concatenate([table[:depth], table[:depth], table[depth:]], axis=0)
    return dot(jnp.concatenate([value_high, value_low, value_high], axis=1), table)


PHASES = (
    (0, 1, 2, 3, 4, 5, 6, 7),
    (8, 9, 10, 11, 12, 13, 14, 15, 16),
)
COUNT = len(PHASES)
WEIGHT_CHUNKS = 4
WAVE_CHUNKS = 3


def front_kernel(
    groups, shards, heads, subs,
    wave_in, target_in, weight_ref, window_in, fourier_in, mel_in, sub_bias_in, gain_in, rel_in,
    qkv_in, lengths_in,
    queries_ref, keys_ref, values_ref, bias_ref,
    wave_ref, target_ref, window_ref, fourier_ref, mel_ref, sub_bias_row, gain_row, rel_ref,
    weights_ref, sub_bias_ref, qkv_ref, lengths_ref, spread_ref,
    *rest,
):
    packed, received, frames = rest[:COUNT], rest[COUNT : 2 * COUNT], rest[2 * COUNT : 3 * COUNT]
    (
        lsem, vsem, wsend, wrecv, ysend, yrecv, fsend, frecv, asend, arecv, hsend, hrecv, nsend, nrecv,
        bsend, brecv, ksend, krecv,
    ) = rest[3 * COUNT :]
    mine = lax.axis_index("groups")
    s, h, u = lax.axis_index("seq"), lax.axis_index("head"), lax.axis_index("sub")
    half = s * subs + u
    halves = shards * subs
    slots = wave_ref.shape[0]
    cap = slots // shards
    depth = weight_ref.shape[0] // (subs * groups * WEIGHT_CHUNKS)

    def place_of(index):
        return {"seq": index // subs, "sub": index % subs}

    def when(condition, action):
        @pl.when(condition)
        def _():
            action()

    pairs = (
        (target_in, target_ref), (window_in, window_ref), (fourier_in, fourier_ref),
        (mel_in, mel_ref), (sub_bias_in, sub_bias_row),
        (gain_in, gain_row), (rel_in, rel_ref), (lengths_in, lengths_ref),
        (weight_ref, weights_ref.at[h]),
        (qkv_in.at[0], qkv_ref.at[0]), (qkv_in.at[1], qkv_ref.at[1]),
        (qkv_in.at[2], qkv_ref.at[2]),
    )
    loads = [pltpu.make_async_copy(a, b, lsem.at[i]) for i, (a, b) in enumerate(pairs)]
    columns = wave_ref.shape[1] // WAVE_CHUNKS
    wave_loads = [
        pltpu.make_async_copy(
            wave_in.at[:, pl.ds(n * columns, columns)],
            wave_ref.at[:, pl.ds(n * columns, columns)],
            vsem.at[n],
        )
        for n in range(WAVE_CHUNKS)
    ]
    for load in loads[:3] + wave_loads + loads[3:8]:
        load.start()

    barrier = pltpu.get_barrier_semaphore()
    for d in range(1, shards):
        pl.semaphore_signal(
            barrier, inc=1, device_id={"seq": lax.rem(s + d, shards)}, device_id_type=MESH
        )
    for d in range(1, heads):
        pl.semaphore_signal(
            barrier, inc=1, device_id={"head": lax.rem(h + d, heads)}, device_id_type=MESH
        )

    for d in range(1, groups):
        pl.semaphore_signal(
            barrier, inc=1, device_id={"groups": lax.rem(mine + d, groups)}, device_id_type=MESH
        )

    @pl.when(half > 0)
    def _():
        pl.semaphore_signal(barrier, inc=1, device_id=place_of(half - 1), device_id_type=MESH)

    @pl.when(half < halves - 1)
    def _():
        pl.semaphore_signal(barrier, inc=1, device_id=place_of(half + 1), device_id_type=MESH)

    sibling = {"sub": lax.rem(u + 1, subs)}

    def weight_rows(group, chunk):
        return pl.ds(((u * groups + group) * WEIGHT_CHUNKS + chunk) * depth, depth)

    def send_weights(source, owner, group, chunk, send_sem, recv_sem, device):
        rows = weight_rows(group, chunk)
        copy = pltpu.make_async_remote_copy(
            src_ref=source.at[rows],
            dst_ref=weights_ref.at[owner, rows],
            send_sem=send_sem,
            recv_sem=recv_sem,
            device_id=device,
            device_id_type=MESH,
        )
        copy.start()
        return copy

    weight_copies, bias_copies = [], []
    loads[0].wait()
    target = target_ref[...]
    owner = jnp.where(target >= 0, lax.shift_right_arithmetic(target, 5), shards)
    place = jnp.bitwise_and(target, PE - 1)
    down = lax.broadcasted_iota(jnp.int32, (slots, slots), 0)
    across = lax.broadcasted_iota(jnp.int32, (slots, slots), 1)
    owner_wide = jnp.broadcast_to(owner, (slots, slots))
    owner_down = jnp.sum(jnp.where(down == across, owner_wide, 0), axis=1, keepdims=True)
    rank = jnp.sum(
        jnp.where((owner_down == owner_wide) & (down < across), 1, 0), axis=0, keepdims=True
    )
    goal = jnp.where(owner < shards, owner * cap + rank, -1)
    chosen = down == goal
    select = chosen.astype(jnp.float32).astype(jnp.bfloat16)
    code = jnp.sum(jnp.where(chosen, place + 1, 0), axis=1, keepdims=True).astype(jnp.float32)
    code = jnp.broadcast_to(code, (slots, LANES)).astype(jnp.bfloat16)

    piece_copies = []
    for index in range(1, 4):
        loads[index].wait()
    loaded = 0
    for phase, frame_numbers in enumerate(PHASES):
        pieces = []
        for f in frame_numbers:
            while loaded * columns < HOP * f + NFFT:
                wave_loads[loaded].wait()
                loaded += 1
            start = HOP * f // LANES * LANES
            if HOP * f == start:
                piece = wave_ref[:, start : start + NFFT]
            else:
                piece = wave_ref[:, start : start + NFFT + LANES]
                piece = pltpu.roll(piece, NFFT + LANES - (HOP * f - start), 1)[:, :NFFT]
            pieces.append(piece * window_ref[...])
        pieces = jnp.concatenate(pieces, axis=0)
        low, high = pieces[:, : NFFT // 2], pieces[:, NFFT // 2 :]
        even = dot_split(low + high, fourier_ref[0])
        odd = dot_split(low - high, fourier_ref[1])
        squares = jnp.concatenate([even * even, odd * odd], axis=1).astype(jnp.bfloat16)
        energy = dot(squares, mel_ref[...])
        logs = jnp.log(1.0 + energy).astype(jnp.bfloat16)
        count = len(frame_numbers)
        logs = jnp.concatenate([logs[n * slots : (n + 1) * slots] for n in range(count)], axis=1)
        rows = dot(select, logs).astype(jnp.bfloat16)
        for t in range(shards):
            packed[phase][t, :, : count * MEL] = rows[t * cap : (t + 1) * cap]
            if phase == 0:
                packed[0][t, :, count * MEL :] = code[t * cap : (t + 1) * cap]
        if phase == 0:
            inner = jnp.where(half > 0, 1, 0) + jnp.where(half < halves - 1, 1, 0)
            pl.semaphore_wait(barrier, shards - 1 + heads - 1 + groups - 1 + inner)
            for chunk in range(WEIGHT_CHUNKS):
                for d in range(1, heads):
                    weight_copies.append(
                        send_weights(
                            weight_ref, h, mine, chunk, wsend.at[chunk, d - 1], wrecv.at[chunk, d - 1],
                            {"head": lax.rem(h + d, heads)},
                        )
                    )
        for d in range(1, shards):
            to = lax.rem(s + d, shards)
            copy = pltpu.make_async_remote_copy(
                src_ref=packed[phase].at[to],
                dst_ref=received[phase].at[s],
                send_sem=asend.at[phase, d - 1],
                recv_sem=arecv.at[phase, d - 1],
                device_id={"seq": to},
                device_id_type=MESH,
            )
            copy.start()
            piece_copies.append(copy)
        received[phase][s] = packed[phase][s]

    for load in loads[8:]:
        load.start()
    loads[4].wait()
    sub_bias_ref[h] = sub_bias_row[...].astype(jnp.float32).reshape(1, sub_bias_row.shape[0])
    for d in range(1, heads):
        copy = pltpu.make_async_remote_copy(
            src_ref=sub_bias_ref.at[h],
            dst_ref=sub_bias_ref.at[h],
            send_sem=bsend.at[d - 1],
            recv_sem=brecv.at[d - 1],
            device_id={"head": lax.rem(h + d, heads)},
            device_id_type=MESH,
        )
        copy.start()
        bias_copies.append(copy)

    across_copies, forward_copies = [], []

    def forward(source, group, chunk, d, index):
        forward_copies.append(
            send_weights(
                weights_ref.at[source], source, group, chunk,
                fsend.at[chunk, d - 1, index], frecv.at[chunk, d - 1, index], sibling,
            )
        )

    def spread_weights(chunk):
        for d in range(1, heads):
            source = lax.rem(h - d + heads, heads)
            weight_copies[chunk * (heads - 1) + d - 1].wait_recv()
            for e in range(1, groups):
                across_copies.append(
                    send_weights(
                        weights_ref.at[source], source, mine, chunk,
                        ysend.at[chunk, d - 1, e - 1], yrecv.at[chunk, d - 1, e - 1],
                        {"groups": lax.rem(mine + e, groups)},
                    )
                )
            forward(source, mine, chunk, d, 0)

    def forward_weights(chunk):
        for d in range(1, heads):
            source = lax.rem(h - d + heads, heads)
            for e in range(1, groups):
                across_copies[(chunk * (heads - 1) + d - 1) * (groups - 1) + e - 1].wait_recv()
                forward(source, lax.rem(mine - e + groups, groups), chunk, d, e)

    @pl.when(half == 0)
    def _():
        for phase in range(COUNT):
            frames[phase][0] = jnp.zeros(frames[phase].shape[1:], jnp.bfloat16)

    @pl.when(half == halves - 1)
    def _():
        for phase in range(COUNT):
            frames[phase][heads + 1] = jnp.zeros(frames[phase].shape[1:], jnp.bfloat16)

    for slot in range(spread_ref.shape[0]):
        spread_ref[slot, PE * FP :] = jnp.zeros((4 * ROWS - PE * FP, MEL), jnp.float32)

    blank_rows = keys_ref.shape[0] - (heads + 2) * ROWS
    for out in (keys_ref, values_ref):
        out[(heads + 2) * ROWS :, :] = jnp.zeros((blank_rows, out.shape[1]), jnp.bfloat16)

    for index in range(5, 8):
        loads[index].wait()
    first_token, token_total = half * heads * CH, halves * heads * CH
    masks = []
    for b in range(heads):
        query_pos = first_token + b * CH + lax.broadcasted_iota(jnp.int32, (CH, 1), 0)
        key_index = lax.broadcasted_iota(jnp.int32, (1, KEYS), 1)
        gap = jnp.zeros_like(key_index)
        for e in range(1, 4):
            gap = gap + (key_index >= e * ROWS).astype(jnp.int32)
        key_in = key_index - gap * ROWS
        key_pos = first_token + (b - 1 + gap) * CH + key_in
        end = jnp.int32(0)
        query_utt = jnp.zeros_like(query_pos)
        key_utt = jnp.zeros_like(key_pos)
        for r in range(lengths_ref.shape[0]):
            end = end + lengths_ref[r]
            query_utt = query_utt + (query_pos >= end).astype(jnp.int32)
            key_utt = key_utt + (key_pos >= end).astype(jnp.int32)
        inside = (key_pos >= 0) & (key_pos < token_total) & (gap < 3) & (key_in < CH)
        key_utt = jnp.where(inside, key_utt, -1)
        masks.append(jnp.where(query_utt == key_utt, 0.0, MASKED))
    taps = rel_ref.shape[1]
    mirror = lax.broadcasted_iota(jnp.int32, (taps, TABLE), 0) + lax.broadcasted_iota(
        jnp.int32, (taps, TABLE), 1
    )
    mirror = (mirror == taps - 1).astype(jnp.float32).astype(jnp.bfloat16)
    rest = rel_ref[...]
    terms = []
    for _ in range(3):
        term = rest.astype(jnp.bfloat16)
        rest = rest - term.astype(jnp.float32)
        terms.append(dot(term, mirror))
    key_lane = lax.broadcasted_iota(jnp.int32, (1, KEYS), 1)
    flipped = terms[0] + (terms[1] + terms[2])
    for row in range(rel_ref.shape[0]):
        wide = jnp.broadcast_to(flipped[row : row + 1, :], (CH, TABLE))
        wide = pltpu.roll(wide, TABLE - (CH - 1), 1, stride=1, stride_axis=0)
        once = pltpu.roll(wide, ROWS - CH, 1)[:, :KEYS]
        twice = pltpu.roll(wide, 2 * (ROWS - CH), 1)[:, :KEYS]
        spaced = jnp.where(
            key_lane < ROWS, wide[:, :KEYS], jnp.where(key_lane < 2 * ROWS, once, twice)
        )
        for b in range(heads):
            bias_ref[row, b] = spaced + masks[b]
        for chunk in range(WEIGHT_CHUNKS):
            if row + 1 == rel_ref.shape[0] * (WEIGHT_CHUNKS + chunk - 1) // (2 * WEIGHT_CHUNKS - 2):
                spread_weights(chunk)

    head_copies = []

    def send_heads(phase):
        for d in range(1, heads):
            copy = pltpu.make_async_remote_copy(
                src_ref=frames[phase].at[h + 1],
                dst_ref=frames[phase].at[h + 1],
                send_sem=hsend.at[phase, d - 1],
                recv_sem=hrecv.at[phase, d - 1],
                device_id={"head": lax.rem(h + d, heads)},
                device_id_type=MESH,
            )
            copy.start()
            head_copies.append(copy)

    def halo(to, source, row, side, phase):
        return pltpu.make_async_remote_copy(
            src_ref=frames[phase].at[source],
            dst_ref=frames[phase].at[row],
            send_sem=nsend.at[phase],
            recv_sem=nrecv.at[phase],
            device_id=place_of(to),
            device_id_type=MESH,
        )

    def halo_up(phase):
        return halo(half + 1, heads, 0, 0, phase)

    def halo_down(phase):
        return halo(half - 1, 1, heads + 1, 1, phase)

    has_up, has_down = (u != 0) & (half < halves - 1), (u == 0) & (half > 0)

    def arrive(phase):
        for d in range(1, shards):
            piece_copies[phase * (shards - 1) + d - 1].wait_recv()
        arrived = received[phase][...]
        if cap % 16:
            arrived = arrived.astype(jnp.float32).reshape(slots, arrived.shape[2])
            return arrived.astype(jnp.bfloat16)
        return arrived.reshape(slots, arrived.shape[2])

    order = None
    for phase, frame_numbers in enumerate(PHASES):
        for chunk in range(WEIGHT_CHUNKS):
            if phase == COUNT - 1:
                forward_weights(chunk)
        arrived = arrive(phase)
        wide = len(frame_numbers) * MEL
        if order is None:
            code_down = arrived[:, wide : wide + 1].astype(jnp.float32)
            code_wide = jnp.broadcast_to(code_down, (slots, slots))
            code_across = jnp.sum(jnp.where(down == across, code_wide, 0.0), axis=0, keepdims=True)
            piece = lax.broadcasted_iota(jnp.int32, (PE, slots), 0).astype(jnp.float32) + 1.0
            order = (piece == code_across).astype(jnp.float32).astype(jnp.bfloat16)
        frames[phase][h + 1] = dot(order, arrived[:, :wide]).astype(jnp.bfloat16)
        send_heads(phase)
        when(has_up & (h == heads - 1), lambda: halo_up(phase).start())
        when(has_down & (h == 0), lambda: halo_down(phase).start())

    for copy in forward_copies + bias_copies:
        copy.wait_recv()
    loads[8].wait()

    def normed_tokens(eighth, slot):
        spread = spread_ref.at[slot]
        for phase, frame_numbers in enumerate(PHASES):
            block = frames[phase][eighth].astype(jnp.float32)
            for n, f in enumerate(frame_numbers):
                spread[pl.ds(f, PE, stride=FP), :] = block[:, n * MEL : (n + 1) * MEL]
        tokens = jnp.concatenate(
            [spread[pl.ds(m, ROWS, stride=4), :] for m in range(4)], axis=1
        ).astype(jnp.bfloat16)
        summed = jnp.concatenate(
            [dot(tokens, weights_ref[g]) + sub_bias_ref[g] for g in range(heads)], axis=1
        )
        value = (summed / (1.0 + jnp.exp(-summed))).astype(jnp.bfloat16).astype(jnp.float32)
        mean = jnp.mean(value, axis=1, keepdims=True)
        centred = value - mean
        variance = jnp.mean(centred * centred, axis=1, keepdims=True)
        gain = gain_row[...].reshape(1, gain_row.shape[0])
        return (centred * lax.rsqrt(variance + EPSILON) * gain).astype(jnp.bfloat16)

    def project(eighth, normed, own):
        if own:
            rows = pl.ds(pl.multiple_of((eighth - 1) * CH, 8), CH)
            queries_ref[rows, :] = dot(normed, qkv_ref[0])[:CH] * (1.0 / math.sqrt(HDIM))
        rows = pl.ds(pl.multiple_of(eighth * ROWS, ROWS), ROWS)
        keys_ref[rows, :] = dot(normed, qkv_ref[1]).astype(jnp.bfloat16)
        values_ref[rows, :] = dot(normed, qkv_ref[2]).astype(jnp.bfloat16)

    def pass_on(phase):
        for d in range(1, heads):
            head_copies[phase * (heads - 1) + d - 1].wait_recv()
        when(has_up & (h != heads - 1), lambda: halo_up(phase).start())
        when(has_down & (h != 0), lambda: halo_down(phase).start())

    normed = normed_tokens(h + 1, 0)
    for phase in range(COUNT - 1):
        pass_on(phase)
    for index in range(9, 12):
        loads[index].wait()
    project(h + 1, normed, True)
    pass_on(COUNT - 1)
    for d in range(1, heads):
        other = lax.rem(h + d, heads) + 1
        project(other, normed_tokens(other, d), True)

    edge = pl.ds(pl.multiple_of(jnp.where(u == 0, heads, 1) * ROWS, ROWS), ROWS)
    landing = pl.ds(pl.multiple_of(jnp.where(u == 0, 0, heads + 1) * ROWS, ROWS), ROWS)
    edge_copies = []
    for index, out in enumerate((keys_ref, values_ref)):
        copy = pltpu.make_async_remote_copy(
            src_ref=out.at[edge],
            dst_ref=out.at[landing],
            send_sem=ksend.at[index],
            recv_sem=krecv.at[index],
            device_id=sibling,
            device_id_type=MESH,
        )
        copy.start()
        edge_copies.append(copy)

    def wait_up():
        for phase in range(COUNT):
            halo_up(phase).wait_recv()

    def wait_down():
        for phase in range(COUNT):
            halo_down(phase).wait_recv()

    when(has_down, wait_up)
    when(has_up, wait_down)
    far = jnp.where(u == 0, 0, heads + 1)
    project(far, normed_tokens(far, heads), False)

    for copy in edge_copies:
        copy.wait()
    for copy in (
        bias_copies + weight_copies + across_copies + forward_copies + piece_copies + head_copies
    ):
        copy.wait_send()
    for phase in range(COUNT):
        when(has_up, lambda: halo_up(phase).wait_send())
        when(has_down, lambda: halo_down(phase).wait_send())


def back_kernel(queries, keys, values, bias_ref, context_out, context_ref, sem):
    blocks = bias_ref.shape[1]
    width = queries.shape[1]
    lane = lax.broadcasted_iota(jnp.int32, (1, LANES), 1)
    ones = jnp.ones((KEYS, LANES), jnp.bfloat16)
    copies = []
    for pair in range(width // LANES):
        lanes = slice(pair * LANES, (pair + 1) * LANES)
        for b in range(blocks):
            query = queries[b * CH : (b + 1) * CH, lanes]
            key = keys[b * ROWS : b * ROWS + KEYS, lanes]
            value = values[b * ROWS : b * ROWS + KEYS, lanes]
            both = jnp.concatenate(
                [jnp.where(lane < HDIM, query, 0.0), jnp.where(lane < HDIM, 0.0, query)], axis=0
            ).astype(jnp.bfloat16)
            scores = lax.dot_general(
                both, key, (((1,), (1,)), ((), ())), preferred_element_type=jnp.float32
            )
            shift = jnp.concatenate([bias_ref[2 * pair, b], bias_ref[2 * pair + 1, b]], axis=0)
            scores = scores + shift
            raised = jnp.exp(scores - jnp.max(scores, axis=1, keepdims=True)).astype(jnp.bfloat16)
            out = dot(raised, jnp.concatenate([value, ones], axis=1))
            out = jnp.where(
                jnp.concatenate([lane, lane], axis=1) % LANES < HDIM, out[:CH], out[CH:]
            )
            joined = out[:, :LANES] / out[:, LANES:]
            context_ref[b * CH : (b + 1) * CH, lanes] = joined.astype(jnp.bfloat16)
        copy = pltpu.make_async_copy(
            context_ref.at[:, lanes], context_out.at[:, lanes], sem.at[pair]
        )
        copy.start()
        copies.append(copy)
    for copy in copies:
        copy.wait()


def local(
    groups, shards, heads, subs,
    wave_pieces, piece_target, utt_lengths, sub_weight, sub_bias, norm_gain, qkv_weight, rel_bias,
):
    slots, samples = wave_pieces.shape[3:]
    cap = slots // shards
    depth, width = sub_weight.shape
    whole_width = qkv_weight.shape[0]
    vmem = pl.BlockSpec(memory_space=pltpu.VMEM)
    sizes = [len(frame_numbers) * MEL for frame_numbers in PHASES]
    payloads = [size + (phase == 0) * MEL for phase, size in enumerate(sizes)]
    dma = pltpu.SemaphoreType.DMA
    hbm = pl.BlockSpec(memory_space=pltpu.HBM)
    heads_here = rel_bias.shape[0]
    tokens_here = heads * CH
    key_rows = (heads - 1) * ROWS + KEYS
    others, parts = heads - 1, WEIGHT_CHUNKS
    queries, keys, values, position_bias = pl.pallas_call(
        functools.partial(front_kernel, groups, shards, heads, subs),
        out_shape=(
            jax.ShapeDtypeStruct((tokens_here, width), jnp.float32),
            jax.ShapeDtypeStruct((key_rows, width), jnp.bfloat16),
            jax.ShapeDtypeStruct((key_rows, width), jnp.bfloat16),
            jax.ShapeDtypeStruct((heads_here, heads, CH, KEYS), jnp.float32),
        ),
        in_specs=[hbm] * 11,
        out_specs=(vmem,) * 4,
        scratch_shapes=[
            pltpu.VMEM((slots, samples), jnp.float32),
            pltpu.VMEM((1, slots), jnp.int32),
            pltpu.VMEM((1, NFFT), jnp.float32),
            pltpu.VMEM((2, NFFT, NFFT // 2), jnp.bfloat16),
            pltpu.VMEM((NFFT, MEL), jnp.bfloat16),
            pltpu.VMEM((width,), jnp.bfloat16),
            pltpu.VMEM((whole_width,), jnp.float32),
            pltpu.VMEM(rel_bias.shape, jnp.float32),
            pltpu.VMEM((heads, depth, width), jnp.bfloat16),
            pltpu.VMEM((heads, 1, width), jnp.float32),
            pltpu.VMEM((3, whole_width, width), jnp.bfloat16),
            pltpu.SMEM(utt_lengths.shape, jnp.int32),
            pltpu.VMEM((heads + 2, 4 * ROWS, MEL), jnp.float32),
            *[pltpu.VMEM((shards, cap, wide), jnp.bfloat16) for wide in payloads],
            *[pltpu.VMEM((shards, cap, wide), jnp.bfloat16) for wide in payloads],
            *[pltpu.VMEM((heads + 2, PE, wide), jnp.bfloat16) for wide in sizes],
            dma((12,)), dma((WAVE_CHUNKS,)),
            dma((parts, others)), dma((parts, others)),
            dma((parts, others, groups - 1)), dma((parts, others, groups - 1)),
            dma((parts, others, groups)), dma((parts, others, groups)),
            dma((COUNT, shards - 1)), dma((COUNT, shards - 1)),
            dma((COUNT, others)), dma((COUNT, others)),
            dma((COUNT,)), dma((COUNT,)), dma((others,)), dma((others,)), dma((2,)), dma((2,)),
        ],
        compiler_params=pltpu.CompilerParams(
            collective_id=0, has_side_effects=True, vmem_limit_bytes=36 << 20
        ),
        name="front",
    )(
        *[
            pltpu.with_memory_space_constraint(value, pltpu.HBM)
            for value in (
                wave_pieces.reshape(slots, samples),
                piece_target.reshape(1, slots),
                sub_weight,
                jnp.asarray(window_table()),
                jnp.asarray(fourier_tables()),
                jnp.asarray(mel_table()),
                sub_bias,
                norm_gain,
                rel_bias,
                jnp.transpose(qkv_weight, (1, 0, 2)),
                utt_lengths,
            )
        ]
    )

    return pl.pallas_call(
        back_kernel,
        out_shape=jax.ShapeDtypeStruct((tokens_here, width), jnp.bfloat16),
        in_specs=[vmem] * 4,
        out_specs=hbm,
        scratch_shapes=[
            pltpu.VMEM((tokens_here, width), jnp.bfloat16),
            dma((width // LANES,)),
        ],
        compiler_params=pltpu.CompilerParams(vmem_limit_bytes=24 << 20),
        name="back",
    )(queries, keys, values, position_bias)


def solution(mesh):
    placed = (
        P(("groups", "seq"), "head", "sub", None, None),
        P(("groups", "seq"), "head", "sub", None),
        P("groups"),
        P(None, "head"),
        P("head"),
        P(),
        P(None, None, "head"),
        P("head", None),
    )
    return jax.shard_map(
        functools.partial(
            local, mesh.shape["groups"], mesh.shape["seq"], mesh.shape["head"], mesh.shape["sub"]
        ),
        mesh=mesh,
        in_specs=placed,
        out_specs=P(("groups", "seq", "sub"), "head"),
        check_vma=False,
    )
```

```python
import functools
import math

import jax
import jax.numpy as jnp
import numpy as np
from jax import lax
from jax.experimental import pallas as pl
from jax.experimental.pallas import tpu as pltpu
from jax.sharding import PartitionSpec as P

HDIM = 64
MEL = 128
NFFT = 512
HOP = 160
FP = 17
CH = 136
PE = 32
LANES = 128
TABLE = 640
KEYS = 512
ROWS = 144


SAMPLE_RATE = 16000.0
EPSILON = 1e-05
MASKED = -1e30
MESH = pl.DeviceIdType.MESH


def split_bf16(table):
    high = table.astype(np.float32).astype(jnp.bfloat16)
    low = (table - high.astype(np.float64)).astype(np.float32).astype(jnp.bfloat16)
    return np.stack([high, low])


def window_table():
    return (0.5 - 0.5 * np.cos(2.0 * np.pi / NFFT * np.arange(NFFT)))[None].astype(np.float32)


def fourier_tables():
    half = NFFT // 2
    sample = np.arange(half)[:, None]

    def phase(bins):
        return (sample * bins[None, :] % NFFT) * (2.0 * np.pi / NFFT)

    even, odd = np.arange(0, half, 2), np.arange(1, half, 2)
    even_sine = np.sin(phase(even))
    even_sine[:, 0] = np.cos(phase(np.array([half])))[:, 0]
    even_table = np.concatenate([np.cos(phase(even)), even_sine], axis=1)
    odd_table = np.concatenate([np.cos(phase(odd)), np.sin(phase(odd))], axis=1)
    return np.stack([np.concatenate(split_bf16(t), axis=0) for t in (even_table, odd_table)])


def mel_table():
    bin_total = NFFT // 2 + 1
    highest = 2595.0 * math.log10(1.0 + SAMPLE_RATE / 2.0 / 700.0)
    points = np.arange(MEL + 2) * (highest / (MEL + 1))
    hertz = 700.0 * (np.power(10.0, points / 2595.0) - 1.0)
    centres = np.arange(bin_total) * (SAMPLE_RATE / NFFT)
    rising = (centres[:, None] - hertz[None, :-2]) / (hertz[1:-1] - hertz[:-2])[None, :]
    falling = (hertz[None, 2:] - centres[:, None]) / (hertz[2:] - hertz[1:-1])[None, :]
    table = np.maximum(0.0, np.minimum(rising, falling))
    sine_even = table[0 : bin_total - 1 : 2].copy()
    sine_even[0] = table[bin_total - 1]
    rows = np.concatenate(
        [table[0 : bin_total - 1 : 2], sine_even, table[1::2], table[1::2]], axis=0
    )
    return rows.astype(np.float32).astype(jnp.bfloat16)


def dot(left, right):
    return jnp.dot(left, right, preferred_element_type=jnp.float32)


def dot_split(value, table):
    value_high = value.astype(jnp.bfloat16)
    value_low = (value - value_high.astype(jnp.float32)).astype(jnp.bfloat16)
    depth = value.shape[1]
    table = jnp.concatenate([table[:depth], table[:depth], table[depth:]], axis=0)
    return dot(jnp.concatenate([value_high, value_low, value_high], axis=1), table)


PHASES = (
    (0, 1, 2, 3, 4, 5, 6, 7),
    (8, 9, 10, 11, 12, 13, 14, 15, 16),
)
COUNT = len(PHASES)
SOLO = 2
WAVE_CHUNKS = 3


def front_kernel(
    groups, shards, heads, subs,
    wave_in, target_in, weight_ref, window_in, fourier_in, mel_in, sub_bias_in, gain_in, rel_in,
    qkv_in, lengths_in,
    queries_ref, keys_ref, values_ref, bias_ref,
    wave_ref, target_ref, window_ref, fourier_ref, mel_ref, sub_bias_row, gain_row, rel_ref,
    weights_ref, sub_bias_ref, qkv_ref, lengths_ref, spread_ref,
    *rest,
):
    packed, received, frames = rest[:COUNT], rest[COUNT : 2 * COUNT], rest[2 * COUNT : 3 * COUNT]
    (
        lsem, vsem, wsend, wrecv, ysend, yrecv, fsend, frecv, asend, arecv, hsend, hrecv, nsend, nrecv,
        bsend, brecv, ksend, krecv,
    ) = rest[3 * COUNT :]
    mine = lax.axis_index("groups")
    s, h, u = lax.axis_index("seq"), lax.axis_index("head"), lax.axis_index("sub")
    half = s * subs + u
    halves = shards * subs
    slots = wave_ref.shape[0]
    cap = slots // shards
    depth = weight_ref.shape[0] // (subs * (groups + SOLO))

    def place_of(index, head):
        return {"seq": index // subs, "sub": index % subs, "head": head}

    def when(condition, action):
        @pl.when(condition)
        def _():
            action()

    pairs = (
        (target_in, target_ref), (window_in, window_ref), (fourier_in, fourier_ref),
        (mel_in, mel_ref), (sub_bias_in, sub_bias_row),
        (gain_in, gain_row), (rel_in, rel_ref), (lengths_in, lengths_ref),
        (weight_ref, weights_ref.at[h]),
        (qkv_in.at[0], qkv_ref.at[0]), (qkv_in.at[1], qkv_ref.at[1]),
        (qkv_in.at[2], qkv_ref.at[2]),
    )
    loads = [pltpu.make_async_copy(a, b, lsem.at[i]) for i, (a, b) in enumerate(pairs)]
    columns = wave_ref.shape[1] // WAVE_CHUNKS
    wave_loads = [
        pltpu.make_async_copy(
            wave_in.at[:, pl.ds(n * columns, columns)],
            wave_ref.at[:, pl.ds(n * columns, columns)],
            vsem.at[n],
        )
        for n in range(WAVE_CHUNKS)
    ]
    for load in loads[:3] + wave_loads + loads[3:8]:
        load.start()

    barrier = pltpu.get_barrier_semaphore()
    for d in range(1, shards):
        pl.semaphore_signal(
            barrier, inc=1, device_id={"seq": lax.rem(s + d, shards)}, device_id_type=MESH
        )
    for d in range(1, heads):
        pl.semaphore_signal(
            barrier, inc=1, device_id={"head": lax.rem(h + d, heads)}, device_id_type=MESH
        )

    for d in range(1, groups):
        pl.semaphore_signal(
            barrier, inc=1, device_id={"groups": lax.rem(mine + d, groups)}, device_id_type=MESH
        )

    sibling = {"sub": lax.rem(u + 1, subs)}
    pl.semaphore_signal(barrier, inc=1, device_id=sibling, device_id_type=MESH)
    far_up, far_down = (u != 0) & (half < halves - 1), (u == 0) & (half > 0)

    @pl.when(far_down)
    def _():
        pl.semaphore_signal(
            barrier, inc=1, device_id=place_of(half - 1, heads - 1), device_id_type=MESH
        )

    @pl.when(far_up)
    def _():
        pl.semaphore_signal(barrier, inc=1, device_id=place_of(half + 1, 0), device_id_type=MESH)

    def send_weights(source, owner, part, send_sem, recv_sem, device):
        rows = pl.ds((u * (groups + SOLO) + part) * depth, depth)
        copy = pltpu.make_async_remote_copy(
            src_ref=source.at[rows],
            dst_ref=weights_ref.at[owner, rows],
            send_sem=send_sem,
            recv_sem=recv_sem,
            device_id=device,
            device_id_type=MESH,
        )
        copy.start()
        return copy

    parts = [mine] + [groups + n for n in range(SOLO)]
    weight_copies, bias_copies = [], []
    loads[0].wait()
    target = target_ref[...]
    owner = jnp.where(target >= 0, lax.shift_right_arithmetic(target, 5), shards)
    place = jnp.bitwise_and(target, PE - 1)
    down = lax.broadcasted_iota(jnp.int32, (slots, slots), 0)
    across = lax.broadcasted_iota(jnp.int32, (slots, slots), 1)
    owner_wide = jnp.broadcast_to(owner, (slots, slots))
    owner_down = jnp.sum(jnp.where(down == across, owner_wide, 0), axis=1, keepdims=True)
    rank = jnp.sum(
        jnp.where((owner_down == owner_wide) & (down < across), 1, 0), axis=0, keepdims=True
    )
    goal = jnp.where(owner < shards, owner * cap + rank, -1)
    chosen = down == goal
    select = chosen.astype(jnp.float32).astype(jnp.bfloat16)
    code = jnp.sum(jnp.where(chosen, place + 1, 0), axis=1, keepdims=True).astype(jnp.float32)
    code = jnp.broadcast_to(code, (slots, LANES)).astype(jnp.bfloat16)

    piece_copies = []
    for index in range(1, 4):
        loads[index].wait()
    loaded = 0
    for phase, frame_numbers in enumerate(PHASES):
        pieces = []
        for f in frame_numbers:
            while loaded * columns < HOP * f + NFFT:
                wave_loads[loaded].wait()
                loaded += 1
            start = HOP * f // LANES * LANES
            if HOP * f == start:
                piece = wave_ref[:, start : start + NFFT]
            else:
                piece = wave_ref[:, start : start + NFFT + LANES]
                piece = pltpu.roll(piece, NFFT + LANES - (HOP * f - start), 1)[:, :NFFT]
            pieces.append(piece * window_ref[...])
        pieces = jnp.concatenate(pieces, axis=0)
        low, high = pieces[:, : NFFT // 2], pieces[:, NFFT // 2 :]
        even = dot_split(low + high, fourier_ref[0])
        odd = dot_split(low - high, fourier_ref[1])
        squares = jnp.concatenate([even * even, odd * odd], axis=1).astype(jnp.bfloat16)
        energy = dot(squares, mel_ref[...])
        logs = jnp.log(1.0 + energy).astype(jnp.bfloat16)
        count = len(frame_numbers)
        logs = jnp.concatenate([logs[n * slots : (n + 1) * slots] for n in range(count)], axis=1)
        rows = dot(select, logs).astype(jnp.bfloat16)
        for t in range(shards):
            packed[phase][t, :, : count * MEL] = rows[t * cap : (t + 1) * cap]
            if phase == 0:
                packed[0][t, :, count * MEL :] = code[t * cap : (t + 1) * cap]
        if phase == 0:
            edges = jnp.where((far_up & (h == heads - 1)) | (far_down & (h == 0)), heads, 0)
            pl.semaphore_wait(barrier, shards - 1 + heads - 1 + groups - 1 + 1 + edges)
            for n, part in enumerate(parts):
                for d in range(1, heads):
                    weight_copies.append(
                        send_weights(
                            weight_ref, h, part, wsend.at[n, d - 1], wrecv.at[n, d - 1],
                            {"head": lax.rem(h + d, heads)},
                        )
                    )
        for d in range(1, shards):
            to = lax.rem(s + d, shards)
            copy = pltpu.make_async_remote_copy(
                src_ref=packed[phase].at[to],
                dst_ref=received[phase].at[s],
                send_sem=asend.at[phase, d - 1],
                recv_sem=arecv.at[phase, d - 1],
                device_id={"seq": to},
                device_id_type=MESH,
            )
            copy.start()
            piece_copies.append(copy)
        received[phase][s] = packed[phase][s]

    for load in loads[8:]:
        load.start()
    loads[4].wait()
    sub_bias_ref[h] = sub_bias_row[...].astype(jnp.float32).reshape(1, sub_bias_row.shape[0])
    for d in range(1, heads):
        copy = pltpu.make_async_remote_copy(
            src_ref=sub_bias_ref.at[h],
            dst_ref=sub_bias_ref.at[h],
            send_sem=bsend.at[d - 1],
            recv_sem=brecv.at[d - 1],
            device_id={"head": lax.rem(h + d, heads)},
            device_id_type=MESH,
        )
        copy.start()
        bias_copies.append(copy)

    across_copies, forward_copies = [], []

    def forward(source, part, d, index):
        forward_copies.append(
            send_weights(
                weights_ref.at[source], source, part,
                fsend.at[d - 1, index], frecv.at[d - 1, index], sibling,
            )
        )

    def spread_weights(n):
        for d in range(1, heads):
            source = lax.rem(h - d + heads, heads)
            weight_copies[n * (heads - 1) + d - 1].wait_recv()
            if n == 0:
                for e in range(1, groups):
                    across_copies.append(
                        send_weights(
                            weights_ref.at[source], source, mine,
                            ysend.at[d - 1, e - 1], yrecv.at[d - 1, e - 1],
                            {"groups": lax.rem(mine + e, groups)},
                        )
                    )
            forward(source, parts[n], d, n)

    def forward_weights():
        for d in range(1, heads):
            source = lax.rem(h - d + heads, heads)
            for e in range(1, groups):
                across_copies[(d - 1) * (groups - 1) + e - 1].wait_recv()
                forward(source, lax.rem(mine - e + groups, groups), d, SOLO + e)

    def clear(start, count):
        for out in (keys_ref, values_ref):
            out[start : start + count, :] = jnp.zeros((count, out.shape[1]), jnp.bfloat16)

    last = (heads + 1) * ROWS
    when(half == 0, lambda: clear(0, ROWS))
    when(half == halves - 1, lambda: clear(last, ROWS))
    clear(last + ROWS, keys_ref.shape[0] - last - ROWS)

    for slot in range(spread_ref.shape[0]):
        spread_ref[slot, PE * FP :] = jnp.zeros((4 * ROWS - PE * FP, MEL), jnp.float32)

    for index in range(5, 8):
        loads[index].wait()
    first_token, token_total = half * heads * CH, halves * heads * CH
    masks = []
    for b in range(heads):
        query_pos = first_token + b * CH + lax.broadcasted_iota(jnp.int32, (CH, 1), 0)
        key_index = lax.broadcasted_iota(jnp.int32, (1, KEYS), 1)
        gap = jnp.zeros_like(key_index)
        for e in range(1, 4):
            gap = gap + (key_index >= e * ROWS).astype(jnp.int32)
        key_in = key_index - gap * ROWS
        key_pos = first_token + (b - 1 + gap) * CH + key_in
        end = jnp.int32(0)
        query_utt = jnp.zeros_like(query_pos)
        key_utt = jnp.zeros_like(key_pos)
        for r in range(lengths_ref.shape[0]):
            end = end + lengths_ref[r]
            query_utt = query_utt + (query_pos >= end).astype(jnp.int32)
            key_utt = key_utt + (key_pos >= end).astype(jnp.int32)
        inside = (key_pos >= 0) & (key_pos < token_total) & (gap < 3) & (key_in < CH)
        key_utt = jnp.where(inside, key_utt, -1)
        masks.append(jnp.where(query_utt == key_utt, 0.0, MASKED))
    taps = rel_ref.shape[1]
    mirror = lax.broadcasted_iota(jnp.int32, (taps, TABLE), 0) + lax.broadcasted_iota(
        jnp.int32, (taps, TABLE), 1
    )
    mirror = (mirror == taps - 1).astype(jnp.float32).astype(jnp.bfloat16)
    rest = rel_ref[...]
    terms = []
    for _ in range(3):
        term = rest.astype(jnp.bfloat16)
        rest = rest - term.astype(jnp.float32)
        terms.append(dot(term, mirror))
    key_lane = lax.broadcasted_iota(jnp.int32, (1, KEYS), 1)
    flipped = terms[0] + (terms[1] + terms[2])
    for row in range(rel_ref.shape[0]):
        wide = jnp.broadcast_to(flipped[row : row + 1, :], (CH, TABLE))
        wide = pltpu.roll(wide, TABLE - (CH - 1), 1, stride=1, stride_axis=0)
        once = pltpu.roll(wide, ROWS - CH, 1)[:, :KEYS]
        twice = pltpu.roll(wide, 2 * (ROWS - CH), 1)[:, :KEYS]
        spaced = jnp.where(
            key_lane < ROWS, wide[:, :KEYS], jnp.where(key_lane < 2 * ROWS, once, twice)
        )
        for b in range(heads):
            bias_ref[row, b] = spaced + masks[b]
        if row + 1 == rel_ref.shape[0] * 2 // 3:
            spread_weights(0)

    spread_weights(1)
    head_copies = []

    def send_heads(phase):
        for d in range(1, heads):
            copy = pltpu.make_async_remote_copy(
                src_ref=frames[phase].at[h + 1],
                dst_ref=frames[phase].at[h + 1],
                send_sem=hsend.at[phase, d - 1],
                recv_sem=hrecv.at[phase, d - 1],
                device_id={"head": lax.rem(h + d, heads)},
                device_id_type=MESH,
            )
            copy.start()
            head_copies.append(copy)

    def halo(to, head, source, row, phase):
        return pltpu.make_async_remote_copy(
            src_ref=frames[phase].at[source],
            dst_ref=frames[phase].at[row],
            send_sem=nsend.at[phase, head],
            recv_sem=nrecv.at[phase],
            device_id=place_of(to, head),
            device_id_type=MESH,
        )

    def halo_up(head, phase):
        return halo(half + 1, head, heads, 0, phase)

    def halo_down(head, phase):
        return halo(half - 1, head, 1, heads + 1, phase)

    def send_far(phase):
        def up():
            for head in range(heads - 1, -1, -1):
                halo_up(head, phase).start()

        def down():
            for head in range(heads):
                halo_down(head, phase).start()

        when(far_up & (h == heads - 1), up)
        when(far_down & (h == 0), down)

    def arrive(phase):
        for d in range(1, shards):
            piece_copies[phase * (shards - 1) + d - 1].wait_recv()
        arrived = received[phase][...]
        if cap % 16:
            arrived = arrived.astype(jnp.float32).reshape(slots, arrived.shape[2])
            return arrived.astype(jnp.bfloat16)
        return arrived.reshape(slots, arrived.shape[2])

    order = None
    for phase, frame_numbers in enumerate(PHASES):
        if phase == COUNT - 1:
            for n in range(2, SOLO + 1):
                spread_weights(n)
            forward_weights()
        arrived = arrive(phase)
        wide = len(frame_numbers) * MEL
        if order is None:
            code_down = arrived[:, wide : wide + 1].astype(jnp.float32)
            code_wide = jnp.broadcast_to(code_down, (slots, slots))
            code_across = jnp.sum(jnp.where(down == across, code_wide, 0.0), axis=0, keepdims=True)
            piece = lax.broadcasted_iota(jnp.int32, (PE, slots), 0).astype(jnp.float32) + 1.0
            order = (piece == code_across).astype(jnp.float32).astype(jnp.bfloat16)
        frames[phase][h + 1] = dot(order, arrived[:, :wide]).astype(jnp.bfloat16)
        send_heads(phase)
        send_far(phase)

    for copy in forward_copies + bias_copies:
        copy.wait_recv()
    loads[8].wait()

    def normed_tokens(eighth, slot):
        spread = spread_ref.at[slot]
        for phase, frame_numbers in enumerate(PHASES):
            block = frames[phase][eighth].astype(jnp.float32)
            for n, f in enumerate(frame_numbers):
                spread[pl.ds(f, PE, stride=FP), :] = block[:, n * MEL : (n + 1) * MEL]
        tokens = jnp.concatenate(
            [spread[pl.ds(m, ROWS, stride=4), :] for m in range(4)], axis=1
        ).astype(jnp.bfloat16)
        summed = jnp.concatenate(
            [dot(tokens, weights_ref[g]) + sub_bias_ref[g] for g in range(heads)], axis=1
        )
        value = (summed / (1.0 + jnp.exp(-summed))).astype(jnp.bfloat16).astype(jnp.float32)
        mean = jnp.mean(value, axis=1, keepdims=True)
        centred = value - mean
        variance = jnp.mean(centred * centred, axis=1, keepdims=True)
        gain = gain_row[...].reshape(1, gain_row.shape[0])
        return (centred * lax.rsqrt(variance + EPSILON) * gain).astype(jnp.bfloat16)

    def project(eighth, normed, own):
        if own:
            rows = pl.ds(pl.multiple_of((eighth - 1) * CH, 8), CH)
            queries_ref[rows, :] = dot(normed, qkv_ref[0])[:CH] * (1.0 / math.sqrt(HDIM))
        rows = pl.ds(pl.multiple_of(eighth * ROWS, ROWS), ROWS)
        keys_ref[rows, :] = dot(normed, qkv_ref[1]).astype(jnp.bfloat16)
        values_ref[rows, :] = dot(normed, qkv_ref[2]).astype(jnp.bfloat16)

    edge = jnp.where(u == 0, heads, 1)
    source_rows = pl.ds(pl.multiple_of(edge * ROWS, ROWS), ROWS)
    landing = pl.ds(pl.multiple_of(jnp.where(u == 0, 0, heads + 1) * ROWS, ROWS), ROWS)
    edge_copies = [
        pltpu.make_async_remote_copy(
            src_ref=out.at[source_rows],
            dst_ref=out.at[landing],
            send_sem=ksend.at[index],
            recv_sem=krecv.at[index],
            device_id=sibling,
            device_id_type=MESH,
        )
        for index, out in enumerate((keys_ref, values_ref))
    ]

    def send_edge():
        for copy in edge_copies:
            copy.start()

    normed = normed_tokens(h + 1, 0)
    for index in range(9, 12):
        loads[index].wait()
    project(h + 1, normed, True)
    when(edge == h + 1, send_edge)
    for copy in bias_copies + weight_copies + across_copies + forward_copies + piece_copies:
        copy.wait_send()
    for d in range(1, heads):
        for phase in range(COUNT):
            head_copies[phase * (heads - 1) + d - 1].wait_recv()
    for d in range(1, heads):
        other = lax.rem(h - d + heads, heads) + 1
        project(other, normed_tokens(other, d), True)
        when(edge == other, send_edge)

    def far_rows():
        row = jnp.where(u == 0, 0, heads + 1)
        for phase in range(COUNT):
            halo(0, 0, 1, row, phase).wait_recv()
        project(row, normed_tokens(row, heads), False)

    when(far_up | far_down, far_rows)

    for copy in edge_copies:
        copy.wait()
    for copy in head_copies:
        copy.wait_send()

    def far_sent(send):
        for phase in range(COUNT):
            for head in range(heads):
                send(head, phase).wait_send()

    when(far_up & (h == heads - 1), lambda: far_sent(halo_up))
    when(far_down & (h == 0), lambda: far_sent(halo_down))


def back_kernel(queries, keys, values, bias_ref, context_out, context_ref, sem):
    blocks = bias_ref.shape[1]
    width = queries.shape[1]
    lane = lax.broadcasted_iota(jnp.int32, (1, LANES), 1)
    ones = jnp.ones((KEYS, LANES), jnp.bfloat16)
    copies = []
    for pair in range(width // LANES):
        lanes = slice(pair * LANES, (pair + 1) * LANES)
        for b in range(blocks):
            query = queries[b * CH : (b + 1) * CH, lanes]
            key = keys[b * ROWS : b * ROWS + KEYS, lanes]
            value = values[b * ROWS : b * ROWS + KEYS, lanes]
            both = jnp.concatenate(
                [jnp.where(lane < HDIM, query, 0.0), jnp.where(lane < HDIM, 0.0, query)], axis=0
            ).astype(jnp.bfloat16)
            scores = lax.dot_general(
                both, key, (((1,), (1,)), ((), ())), preferred_element_type=jnp.float32
            )
            shift = jnp.concatenate([bias_ref[2 * pair, b], bias_ref[2 * pair + 1, b]], axis=0)
            scores = scores + shift
            raised = jnp.exp(scores - jnp.max(scores, axis=1, keepdims=True)).astype(jnp.bfloat16)
            out = dot(raised, jnp.concatenate([value, ones], axis=1))
            out = jnp.where(
                jnp.concatenate([lane, lane], axis=1) % LANES < HDIM, out[:CH], out[CH:]
            )
            joined = out[:, :LANES] / out[:, LANES:]
            context_ref[b * CH : (b + 1) * CH, lanes] = joined.astype(jnp.bfloat16)
        copy = pltpu.make_async_copy(
            context_ref.at[:, lanes], context_out.at[:, lanes], sem.at[pair]
        )
        copy.start()
        copies.append(copy)
    for copy in copies:
        copy.wait()


def local(
    groups, shards, heads, subs,
    wave_pieces, piece_target, utt_lengths, sub_weight, sub_bias, norm_gain, qkv_weight, rel_bias,
):
    slots, samples = wave_pieces.shape[3:]
    cap = slots // shards
    depth, width = sub_weight.shape
    whole_width = qkv_weight.shape[0]
    vmem = pl.BlockSpec(memory_space=pltpu.VMEM)
    sizes = [len(frame_numbers) * MEL for frame_numbers in PHASES]
    payloads = [size + (phase == 0) * MEL for phase, size in enumerate(sizes)]
    dma = pltpu.SemaphoreType.DMA
    hbm = pl.BlockSpec(memory_space=pltpu.HBM)
    heads_here = rel_bias.shape[0]
    tokens_here = heads * CH
    key_rows = (heads - 1) * ROWS + KEYS
    others = heads - 1
    queries, keys, values, position_bias = pl.pallas_call(
        functools.partial(front_kernel, groups, shards, heads, subs),
        out_shape=(
            jax.ShapeDtypeStruct((tokens_here, width), jnp.float32),
            jax.ShapeDtypeStruct((key_rows, width), jnp.bfloat16),
            jax.ShapeDtypeStruct((key_rows, width), jnp.bfloat16),
            jax.ShapeDtypeStruct((heads_here, heads, CH, KEYS), jnp.float32),
        ),
        in_specs=[hbm] * 11,
        out_specs=(vmem,) * 4,
        scratch_shapes=[
            pltpu.VMEM((slots, samples), jnp.float32),
            pltpu.VMEM((1, slots), jnp.int32),
            pltpu.VMEM((1, NFFT), jnp.float32),
            pltpu.VMEM((2, NFFT, NFFT // 2), jnp.bfloat16),
            pltpu.VMEM((NFFT, MEL), jnp.bfloat16),
            pltpu.VMEM((width,), jnp.bfloat16),
            pltpu.VMEM((whole_width,), jnp.float32),
            pltpu.VMEM(rel_bias.shape, jnp.float32),
            pltpu.VMEM((heads, depth, width), jnp.bfloat16),
            pltpu.VMEM((heads, 1, width), jnp.float32),
            pltpu.VMEM((3, whole_width, width), jnp.bfloat16),
            pltpu.SMEM(utt_lengths.shape, jnp.int32),
            pltpu.VMEM((heads + 1, 4 * ROWS, MEL), jnp.float32),
            *[pltpu.VMEM((shards, cap, wide), jnp.bfloat16) for wide in payloads],
            *[pltpu.VMEM((shards, cap, wide), jnp.bfloat16) for wide in payloads],
            *[pltpu.VMEM((heads + 2, PE, wide), jnp.bfloat16) for wide in sizes],
            dma((12,)), dma((WAVE_CHUNKS,)),
            dma((SOLO + 1, others)), dma((SOLO + 1, others)),
            dma((others, groups - 1)), dma((others, groups - 1)),
            dma((others, groups + SOLO)), dma((others, groups + SOLO)),
            dma((COUNT, shards - 1)), dma((COUNT, shards - 1)),
            dma((COUNT, others)), dma((COUNT, others)),
            dma((COUNT, heads)), dma((COUNT,)), dma((others,)), dma((others,)), dma((2,)), dma((2,)),
        ],
        compiler_params=pltpu.CompilerParams(
            collective_id=0, has_side_effects=True, vmem_limit_bytes=36 << 20
        ),
        name="front",
    )(
        *[
            pltpu.with_memory_space_constraint(value, pltpu.HBM)
            for value in (
                wave_pieces.reshape(slots, samples),
                piece_target.reshape(1, slots),
                sub_weight,
                jnp.asarray(window_table()),
                jnp.asarray(fourier_tables()),
                jnp.asarray(mel_table()),
                sub_bias,
                norm_gain,
                rel_bias,
                jnp.transpose(qkv_weight, (1, 0, 2)),
                utt_lengths,
            )
        ]
    )

    return pl.pallas_call(
        back_kernel,
        out_shape=jax.ShapeDtypeStruct((tokens_here, width), jnp.bfloat16),
        in_specs=[vmem] * 4,
        out_specs=hbm,
        scratch_shapes=[
            pltpu.VMEM((tokens_here, width), jnp.bfloat16),
            dma((width // LANES,)),
        ],
        compiler_params=pltpu.CompilerParams(vmem_limit_bytes=24 << 20),
        name="back",
    )(queries, keys, values, position_bias)


def solution(mesh):
    placed = (
        P(("groups", "seq"), "head", "sub", None, None),
        P(("groups", "seq"), "head", "sub", None),
        P("groups"),
        P(None, "head"),
        P("head"),
        P(),
        P(None, None, "head"),
        P("head", None),
    )
    return jax.shard_map(
        functools.partial(
            local, mesh.shape["groups"], mesh.shape["seq"], mesh.shape["head"], mesh.shape["sub"]
        ),
        mesh=mesh,
        in_specs=placed,
        out_specs=P(("groups", "seq", "sub"), "head"),
        check_vma=False,
    )
```

```python
import functools
import math

import jax
import jax.numpy as jnp
import numpy as np
from jax import lax
from jax.experimental import pallas as pl
from jax.experimental.pallas import tpu as pltpu
from jax.sharding import PartitionSpec as P

HDIM = 64
MEL = 128
NFFT = 512
HOP = 160
FP = 17
CH = 136
PE = 32
LANES = 128
TABLE = 640
KEYS = 512
ROWS = 144


SAMPLE_RATE = 16000.0
EPSILON = 1e-05
MASKED = -1e30
MESH = pl.DeviceIdType.MESH


def split_bf16(table):
    high = table.astype(np.float32).astype(jnp.bfloat16)
    low = (table - high.astype(np.float64)).astype(np.float32).astype(jnp.bfloat16)
    return np.stack([high, low])


def window_table():
    return (0.5 - 0.5 * np.cos(2.0 * np.pi / NFFT * np.arange(NFFT)))[None].astype(np.float32)


def fourier_tables():
    half = NFFT // 2
    sample = np.arange(half)[:, None]

    def phase(bins):
        return (sample * bins[None, :] % NFFT) * (2.0 * np.pi / NFFT)

    even, odd = np.arange(0, half, 2), np.arange(1, half, 2)
    even_sine = np.sin(phase(even))
    even_sine[:, 0] = np.cos(phase(np.array([half])))[:, 0]
    even_table = np.concatenate([np.cos(phase(even)), even_sine], axis=1)
    odd_table = np.concatenate([np.cos(phase(odd)), np.sin(phase(odd))], axis=1)
    return np.stack([np.concatenate(split_bf16(t), axis=0) for t in (even_table, odd_table)])


def mel_table():
    bin_total = NFFT // 2 + 1
    highest = 2595.0 * math.log10(1.0 + SAMPLE_RATE / 2.0 / 700.0)
    points = np.arange(MEL + 2) * (highest / (MEL + 1))
    hertz = 700.0 * (np.power(10.0, points / 2595.0) - 1.0)
    centres = np.arange(bin_total) * (SAMPLE_RATE / NFFT)
    rising = (centres[:, None] - hertz[None, :-2]) / (hertz[1:-1] - hertz[:-2])[None, :]
    falling = (hertz[None, 2:] - centres[:, None]) / (hertz[2:] - hertz[1:-1])[None, :]
    table = np.maximum(0.0, np.minimum(rising, falling))
    sine_even = table[0 : bin_total - 1 : 2].copy()
    sine_even[0] = table[bin_total - 1]
    rows = np.concatenate(
        [table[0 : bin_total - 1 : 2], sine_even, table[1::2], table[1::2]], axis=0
    )
    return rows.astype(np.float32).astype(jnp.bfloat16)


def dot(left, right):
    return jnp.dot(left, right, preferred_element_type=jnp.float32)


def dot_split(value, table):
    value_high = value.astype(jnp.bfloat16)
    value_low = (value - value_high.astype(jnp.float32)).astype(jnp.bfloat16)
    depth = value.shape[1]
    table = jnp.concatenate([table[:depth], table[:depth], table[depth:]], axis=0)
    return dot(jnp.concatenate([value_high, value_low, value_high], axis=1), table)


PHASES = (
    (0, 1, 2, 3, 4, 5, 6, 7),
    (8, 9, 10, 11, 12, 13, 14, 15, 16),
)
COUNT = len(PHASES)
SOLO = 2
WAVE_CHUNKS = 3


def front_kernel(
    groups, shards, heads, subs,
    wave_in, target_in, weight_ref, window_in, fourier_in, mel_in, sub_bias_in, gain_in, rel_in,
    qkv_in, lengths_in,
    queries_ref, keys_ref, values_ref, bias_ref,
    wave_ref, target_ref, window_ref, fourier_ref, mel_ref, sub_bias_row, gain_row, rel_ref,
    weights_ref, sub_bias_ref, qkv_ref, lengths_ref, spread_ref,
    *rest,
):
    packed, received, frames = rest[:COUNT], rest[COUNT : 2 * COUNT], rest[2 * COUNT : 3 * COUNT]
    (
        lsem, vsem, wsend, wrecv, ysend, yrecv, fsend, frecv, asend, arecv, hsend, hrecv, nsend, nrecv,
        bsend, brecv, ksend, krecv,
    ) = rest[3 * COUNT :]
    mine = lax.axis_index("groups")
    s, h, u = lax.axis_index("seq"), lax.axis_index("head"), lax.axis_index("sub")
    half = s * subs + u
    halves = shards * subs
    slots = wave_ref.shape[0]
    cap = slots // shards
    depth = weight_ref.shape[0] // (subs * (groups + SOLO))

    def place_of(index, head):
        return {"seq": index // subs, "sub": index % subs, "head": head}

    def when(condition, action):
        @pl.when(condition)
        def _():
            action()

    pairs = (
        (target_in, target_ref), (window_in, window_ref), (fourier_in, fourier_ref),
        (mel_in, mel_ref), (sub_bias_in, sub_bias_row),
        (gain_in, gain_row), (rel_in, rel_ref), (lengths_in, lengths_ref),
        (weight_ref, weights_ref.at[h]),
        (qkv_in.at[0], qkv_ref.at[0]), (qkv_in.at[1], qkv_ref.at[1]),
        (qkv_in.at[2], qkv_ref.at[2]),
    )
    loads = [pltpu.make_async_copy(a, b, lsem.at[i]) for i, (a, b) in enumerate(pairs)]
    columns = wave_ref.shape[1] // WAVE_CHUNKS
    wave_loads = [
        pltpu.make_async_copy(
            wave_in.at[:, pl.ds(n * columns, columns)],
            wave_ref.at[:, pl.ds(n * columns, columns)],
            vsem.at[n],
        )
        for n in range(WAVE_CHUNKS)
    ]
    for load in loads[:3] + wave_loads + loads[3:8]:
        load.start()

    barrier = pltpu.get_barrier_semaphore()
    for d in range(1, shards):
        pl.semaphore_signal(
            barrier, inc=1, device_id={"seq": lax.rem(s + d, shards)}, device_id_type=MESH
        )
    for d in range(1, heads):
        pl.semaphore_signal(
            barrier, inc=1, device_id={"head": lax.rem(h + d, heads)}, device_id_type=MESH
        )

    for d in range(1, groups):
        pl.semaphore_signal(
            barrier, inc=1, device_id={"groups": lax.rem(mine + d, groups)}, device_id_type=MESH
        )

    sibling = {"sub": lax.rem(u + 1, subs)}
    pl.semaphore_signal(barrier, inc=1, device_id=sibling, device_id_type=MESH)
    far_up, far_down = (u != 0) & (half < halves - 1), (u == 0) & (half > 0)

    @pl.when(far_down)
    def _():
        pl.semaphore_signal(
            barrier, inc=1, device_id=place_of(half - 1, heads - 1), device_id_type=MESH
        )

    @pl.when(far_up)
    def _():
        pl.semaphore_signal(barrier, inc=1, device_id=place_of(half + 1, 0), device_id_type=MESH)

    def send_weights(source, owner, part, send_sem, recv_sem, device):
        rows = pl.ds((u * (groups + SOLO) + part) * depth, depth)
        copy = pltpu.make_async_remote_copy(
            src_ref=source.at[rows],
            dst_ref=weights_ref.at[owner, rows],
            send_sem=send_sem,
            recv_sem=recv_sem,
            device_id=device,
            device_id_type=MESH,
        )
        copy.start()
        return copy

    parts = [mine] + [groups + n for n in range(SOLO)]
    weight_copies, bias_copies = [], []
    loads[0].wait()
    target = target_ref[...]
    owner = jnp.where(target >= 0, lax.shift_right_arithmetic(target, 5), shards)
    place = jnp.bitwise_and(target, PE - 1)
    down = lax.broadcasted_iota(jnp.int32, (slots, slots), 0)
    across = lax.broadcasted_iota(jnp.int32, (slots, slots), 1)
    owner_wide = jnp.broadcast_to(owner, (slots, slots))
    owner_down = jnp.sum(jnp.where(down == across, owner_wide, 0), axis=1, keepdims=True)
    rank = jnp.sum(
        jnp.where((owner_down == owner_wide) & (down < across), 1, 0), axis=0, keepdims=True
    )
    goal = jnp.where(owner < shards, owner * cap + rank, -1)
    chosen = down == goal
    select = chosen.astype(jnp.float32).astype(jnp.bfloat16)
    code = jnp.sum(jnp.where(chosen, place + 1, 0), axis=1, keepdims=True).astype(jnp.float32)
    code = jnp.broadcast_to(code, (slots, LANES)).astype(jnp.bfloat16)

    piece_copies = []
    for index in range(1, 4):
        loads[index].wait()
    loaded = 0
    for phase, frame_numbers in enumerate(PHASES):
        pieces = []
        for f in frame_numbers:
            while loaded * columns < HOP * f + NFFT:
                wave_loads[loaded].wait()
                loaded += 1
            start = HOP * f // LANES * LANES
            if HOP * f == start:
                piece = wave_ref[:, start : start + NFFT]
            else:
                piece = wave_ref[:, start : start + NFFT + LANES]
                piece = pltpu.roll(piece, NFFT + LANES - (HOP * f - start), 1)[:, :NFFT]
            pieces.append(piece * window_ref[...])
        pieces = jnp.concatenate(pieces, axis=0)
        low, high = pieces[:, : NFFT // 2], pieces[:, NFFT // 2 :]
        even = dot_split(low + high, fourier_ref[0])
        odd = dot_split(low - high, fourier_ref[1])
        squares = jnp.concatenate([even * even, odd * odd], axis=1).astype(jnp.bfloat16)
        energy = dot(squares, mel_ref[...])
        logs = jnp.log(1.0 + energy).astype(jnp.bfloat16)
        count = len(frame_numbers)
        logs = jnp.concatenate([logs[n * slots : (n + 1) * slots] for n in range(count)], axis=1)
        rows = dot(select, logs).astype(jnp.bfloat16)
        for t in range(shards):
            packed[phase][t, :, : count * MEL] = rows[t * cap : (t + 1) * cap]
            if phase == 0:
                packed[0][t, :, count * MEL :] = code[t * cap : (t + 1) * cap]
        if phase == 0:
            edges = jnp.where((far_up & (h == heads - 1)) | (far_down & (h == 0)), heads, 0)
            pl.semaphore_wait(barrier, shards - 1 + heads - 1 + groups - 1 + 1 + edges)
            for n, part in enumerate(parts):
                for d in range(1, heads):
                    weight_copies.append(
                        send_weights(
                            weight_ref, h, part, wsend.at[n, d - 1], wrecv.at[n, d - 1],
                            {"head": lax.rem(h + d, heads)},
                        )
                    )
        for d in range(1, shards):
            to = lax.rem(s + d, shards)
            copy = pltpu.make_async_remote_copy(
                src_ref=packed[phase].at[to],
                dst_ref=received[phase].at[s],
                send_sem=asend.at[phase, d - 1],
                recv_sem=arecv.at[phase, d - 1],
                device_id={"seq": to},
                device_id_type=MESH,
            )
            copy.start()
            piece_copies.append(copy)
        received[phase][s] = packed[phase][s]

    for load in loads[8:]:
        load.start()
    loads[4].wait()
    sub_bias_ref[h] = sub_bias_row[...].astype(jnp.float32).reshape(1, sub_bias_row.shape[0])
    for d in range(1, heads):
        copy = pltpu.make_async_remote_copy(
            src_ref=sub_bias_ref.at[h],
            dst_ref=sub_bias_ref.at[h],
            send_sem=bsend.at[d - 1],
            recv_sem=brecv.at[d - 1],
            device_id={"head": lax.rem(h + d, heads)},
            device_id_type=MESH,
        )
        copy.start()
        bias_copies.append(copy)

    across_copies, forward_copies = [], []

    def forward(source, part, d, index):
        forward_copies.append(
            send_weights(
                weights_ref.at[source], source, part,
                fsend.at[d - 1, index], frecv.at[d - 1, index], sibling,
            )
        )

    def spread_weights(n):
        for d in range(1, heads):
            source = lax.rem(h - d + heads, heads)
            weight_copies[n * (heads - 1) + d - 1].wait_recv()
            if n == 0:
                for e in range(1, groups):
                    across_copies.append(
                        send_weights(
                            weights_ref.at[source], source, mine,
                            ysend.at[d - 1, e - 1], yrecv.at[d - 1, e - 1],
                            {"groups": lax.rem(mine + e, groups)},
                        )
                    )
            forward(source, parts[n], d, n)

    def forward_weights():
        for d in range(1, heads):
            source = lax.rem(h - d + heads, heads)
            for e in range(1, groups):
                across_copies[(d - 1) * (groups - 1) + e - 1].wait_recv()
                forward(source, lax.rem(mine - e + groups, groups), d, SOLO + e)

    def clear(start, count):
        for out in (keys_ref, values_ref):
            out[start : start + count, :] = jnp.zeros((count, out.shape[1]), jnp.bfloat16)

    last = (heads + 1) * ROWS
    when(half == 0, lambda: clear(0, ROWS))
    when(half == halves - 1, lambda: clear(last, ROWS))
    clear(last + ROWS, keys_ref.shape[0] - last - ROWS)

    for slot in range(spread_ref.shape[0]):
        spread_ref[slot, PE * FP :] = jnp.zeros((4 * ROWS - PE * FP, MEL), jnp.float32)

    for index in range(5, 8):
        loads[index].wait()
    first_token, token_total = half * heads * CH, halves * heads * CH
    masks = []
    for b in range(heads):
        query_pos = first_token + b * CH + lax.broadcasted_iota(jnp.int32, (CH, 1), 0)
        key_index = lax.broadcasted_iota(jnp.int32, (1, KEYS), 1)
        gap = jnp.zeros_like(key_index)
        for e in range(1, 4):
            gap = gap + (key_index >= e * ROWS).astype(jnp.int32)
        key_in = key_index - gap * ROWS
        key_pos = first_token + (b - 1 + gap) * CH + key_in
        end = jnp.int32(0)
        query_utt = jnp.zeros_like(query_pos)
        key_utt = jnp.zeros_like(key_pos)
        for r in range(lengths_ref.shape[0]):
            end = end + lengths_ref[r]
            query_utt = query_utt + (query_pos >= end).astype(jnp.int32)
            key_utt = key_utt + (key_pos >= end).astype(jnp.int32)
        inside = (key_pos >= 0) & (key_pos < token_total) & (gap < 3) & (key_in < CH)
        key_utt = jnp.where(inside, key_utt, -1)
        masks.append(jnp.where(query_utt == key_utt, 0.0, MASKED))
    taps = rel_ref.shape[1]
    mirror = lax.broadcasted_iota(jnp.int32, (taps, TABLE), 0) + lax.broadcasted_iota(
        jnp.int32, (taps, TABLE), 1
    )
    mirror = (mirror == taps - 1).astype(jnp.float32).astype(jnp.bfloat16)
    rest = rel_ref[...]
    terms = []
    for _ in range(3):
        term = rest.astype(jnp.bfloat16)
        rest = rest - term.astype(jnp.float32)
        terms.append(dot(term, mirror))
    key_lane = lax.broadcasted_iota(jnp.int32, (1, KEYS), 1)
    flipped = terms[0] + (terms[1] + terms[2])
    for row in range(rel_ref.shape[0]):
        wide = jnp.broadcast_to(flipped[row : row + 1, :], (CH, TABLE))
        wide = pltpu.roll(wide, TABLE - (CH - 1), 1, stride=1, stride_axis=0)
        once = pltpu.roll(wide, ROWS - CH, 1)[:, :KEYS]
        twice = pltpu.roll(wide, 2 * (ROWS - CH), 1)[:, :KEYS]
        spaced = jnp.where(
            key_lane < ROWS, wide[:, :KEYS], jnp.where(key_lane < 2 * ROWS, once, twice)
        )
        for b in range(heads):
            bias_ref[row, b] = spaced + masks[b]
        if row + 1 == rel_ref.shape[0] * 2 // 3:
            spread_weights(0)

    spread_weights(1)
    head_copies = []

    def send_heads(phase):
        for d in range(1, heads):
            copy = pltpu.make_async_remote_copy(
                src_ref=frames[phase].at[h + 1],
                dst_ref=frames[phase].at[h + 1],
                send_sem=hsend.at[phase, d - 1],
                recv_sem=hrecv.at[phase, d - 1],
                device_id={"head": lax.rem(h + d, heads)},
                device_id_type=MESH,
            )
            copy.start()
            head_copies.append(copy)

    def halo(to, head, source, row, phase):
        return pltpu.make_async_remote_copy(
            src_ref=frames[phase].at[source],
            dst_ref=frames[phase].at[row],
            send_sem=nsend.at[phase, head],
            recv_sem=nrecv.at[phase],
            device_id=place_of(to, head),
            device_id_type=MESH,
        )

    def halo_up(head, phase):
        return halo(half + 1, head, heads, 0, phase)

    def halo_down(head, phase):
        return halo(half - 1, head, 1, heads + 1, phase)

    def send_far(phase):
        def up():
            for head in range(heads - 1, -1, -1):
                halo_up(head, phase).start()

        def down():
            for head in range(heads):
                halo_down(head, phase).start()

        when(far_up & (h == heads - 1), up)
        when(far_down & (h == 0), down)

    def arrive(phase):
        for d in range(1, shards):
            piece_copies[phase * (shards - 1) + d - 1].wait_recv()
        arrived = received[phase][...]
        if cap % 16:
            arrived = arrived.astype(jnp.float32).reshape(slots, arrived.shape[2])
            return arrived.astype(jnp.bfloat16)
        return arrived.reshape(slots, arrived.shape[2])

    order = None
    for phase, frame_numbers in enumerate(PHASES):
        if phase == COUNT - 1:
            for n in range(2, SOLO + 1):
                spread_weights(n)
            forward_weights()
        arrived = arrive(phase)
        wide = len(frame_numbers) * MEL
        if order is None:
            code_down = arrived[:, wide : wide + 1].astype(jnp.float32)
            code_wide = jnp.broadcast_to(code_down, (slots, slots))
            code_across = jnp.sum(jnp.where(down == across, code_wide, 0.0), axis=0, keepdims=True)
            piece = lax.broadcasted_iota(jnp.int32, (PE, slots), 0).astype(jnp.float32) + 1.0
            order = (piece == code_across).astype(jnp.float32).astype(jnp.bfloat16)
        frames[phase][h + 1] = dot(order, arrived[:, :wide]).astype(jnp.bfloat16)
        send_heads(phase)
        if phase < COUNT - 1:
            send_far(phase)

    for copy in forward_copies + bias_copies:
        copy.wait_recv()
    loads[8].wait()

    def normed_tokens(eighth, slot):
        spread = spread_ref.at[slot]
        for phase, frame_numbers in enumerate(PHASES):
            block = frames[phase][eighth].astype(jnp.float32)
            for n, f in enumerate(frame_numbers):
                spread[pl.ds(f, PE, stride=FP), :] = block[:, n * MEL : (n + 1) * MEL]
        tokens = jnp.concatenate(
            [spread[pl.ds(m, ROWS, stride=4), :] for m in range(4)], axis=1
        ).astype(jnp.bfloat16)
        summed = jnp.concatenate(
            [dot(tokens, weights_ref[g]) + sub_bias_ref[g] for g in range(heads)], axis=1
        )
        value = (summed / (1.0 + jnp.exp(-summed))).astype(jnp.bfloat16).astype(jnp.float32)
        mean = jnp.mean(value, axis=1, keepdims=True)
        centred = value - mean
        variance = jnp.mean(centred * centred, axis=1, keepdims=True)
        gain = gain_row[...].reshape(1, gain_row.shape[0])
        return (centred * lax.rsqrt(variance + EPSILON) * gain).astype(jnp.bfloat16)

    def project(eighth, normed, own):
        if own:
            rows = pl.ds(pl.multiple_of((eighth - 1) * CH, 8), CH)
            queries_ref[rows, :] = dot(normed, qkv_ref[0])[:CH] * (1.0 / math.sqrt(HDIM))
        rows = pl.ds(pl.multiple_of(eighth * ROWS, ROWS), ROWS)
        keys_ref[rows, :] = dot(normed, qkv_ref[1]).astype(jnp.bfloat16)
        values_ref[rows, :] = dot(normed, qkv_ref[2]).astype(jnp.bfloat16)

    edge = jnp.where(u == 0, heads, 1)
    source_rows = pl.ds(pl.multiple_of(edge * ROWS, ROWS), ROWS)
    landing = pl.ds(pl.multiple_of(jnp.where(u == 0, 0, heads + 1) * ROWS, ROWS), ROWS)
    edge_copies = [
        pltpu.make_async_remote_copy(
            src_ref=out.at[source_rows],
            dst_ref=out.at[landing],
            send_sem=ksend.at[index],
            recv_sem=krecv.at[index],
            device_id=sibling,
            device_id_type=MESH,
        )
        for index, out in enumerate((keys_ref, values_ref))
    ]

    def send_edge():
        for copy in edge_copies:
            copy.start()

    normed = normed_tokens(h + 1, 0)
    send_far(COUNT - 1)
    for index in range(9, 12):
        loads[index].wait()
    project(h + 1, normed, True)
    when(edge == h + 1, send_edge)
    for copy in bias_copies + weight_copies + across_copies + forward_copies + piece_copies:
        copy.wait_send()
    for d in range(1, heads):
        for phase in range(COUNT):
            head_copies[phase * (heads - 1) + d - 1].wait_recv()
    for d in range(1, heads):
        other = lax.rem(h - d + heads, heads) + 1
        project(other, normed_tokens(other, d), True)
        when(edge == other, send_edge)

    def far_rows():
        row = jnp.where(u == 0, 0, heads + 1)
        for phase in range(COUNT):
            halo(0, 0, 1, row, phase).wait_recv()
        project(row, normed_tokens(row, heads), False)

    when(far_up | far_down, far_rows)

    for copy in edge_copies:
        copy.wait()
    for copy in head_copies:
        copy.wait_send()

    def far_sent(send):
        for phase in range(COUNT):
            for head in range(heads):
                send(head, phase).wait_send()

    when(far_up & (h == heads - 1), lambda: far_sent(halo_up))
    when(far_down & (h == 0), lambda: far_sent(halo_down))


def back_kernel(queries, keys, values, bias_ref, context_out, context_ref, sem):
    blocks = bias_ref.shape[1]
    width = queries.shape[1]
    lane = lax.broadcasted_iota(jnp.int32, (1, LANES), 1)
    ones = jnp.ones((KEYS, LANES), jnp.bfloat16)
    copies = []
    for pair in range(width // LANES):
        lanes = slice(pair * LANES, (pair + 1) * LANES)
        for b in range(blocks):
            query = queries[b * CH : (b + 1) * CH, lanes]
            key = keys[b * ROWS : b * ROWS + KEYS, lanes]
            value = values[b * ROWS : b * ROWS + KEYS, lanes]
            both = jnp.concatenate(
                [jnp.where(lane < HDIM, query, 0.0), jnp.where(lane < HDIM, 0.0, query)], axis=0
            ).astype(jnp.bfloat16)
            scores = lax.dot_general(
                both, key, (((1,), (1,)), ((), ())), preferred_element_type=jnp.float32
            )
            shift = jnp.concatenate([bias_ref[2 * pair, b], bias_ref[2 * pair + 1, b]], axis=0)
            scores = scores + shift
            raised = jnp.exp(scores - jnp.max(scores, axis=1, keepdims=True)).astype(jnp.bfloat16)
            out = dot(raised, jnp.concatenate([value, ones], axis=1))
            out = jnp.where(
                jnp.concatenate([lane, lane], axis=1) % LANES < HDIM, out[:CH], out[CH:]
            )
            joined = out[:, :LANES] / out[:, LANES:]
            context_ref[b * CH : (b + 1) * CH, lanes] = joined.astype(jnp.bfloat16)
        copy = pltpu.make_async_copy(
            context_ref.at[:, lanes], context_out.at[:, lanes], sem.at[pair]
        )
        copy.start()
        copies.append(copy)
    for copy in copies:
        copy.wait()


def local(
    groups, shards, heads, subs,
    wave_pieces, piece_target, utt_lengths, sub_weight, sub_bias, norm_gain, qkv_weight, rel_bias,
):
    slots, samples = wave_pieces.shape[3:]
    cap = slots // shards
    depth, width = sub_weight.shape
    whole_width = qkv_weight.shape[0]
    vmem = pl.BlockSpec(memory_space=pltpu.VMEM)
    sizes = [len(frame_numbers) * MEL for frame_numbers in PHASES]
    payloads = [size + (phase == 0) * MEL for phase, size in enumerate(sizes)]
    dma = pltpu.SemaphoreType.DMA
    hbm = pl.BlockSpec(memory_space=pltpu.HBM)
    heads_here = rel_bias.shape[0]
    tokens_here = heads * CH
    key_rows = (heads - 1) * ROWS + KEYS
    others = heads - 1
    queries, keys, values, position_bias = pl.pallas_call(
        functools.partial(front_kernel, groups, shards, heads, subs),
        out_shape=(
            jax.ShapeDtypeStruct((tokens_here, width), jnp.float32),
            jax.ShapeDtypeStruct((key_rows, width), jnp.bfloat16),
            jax.ShapeDtypeStruct((key_rows, width), jnp.bfloat16),
            jax.ShapeDtypeStruct((heads_here, heads, CH, KEYS), jnp.float32),
        ),
        in_specs=[hbm] * 11,
        out_specs=(vmem,) * 4,
        scratch_shapes=[
            pltpu.VMEM((slots, samples), jnp.float32),
            pltpu.VMEM((1, slots), jnp.int32),
            pltpu.VMEM((1, NFFT), jnp.float32),
            pltpu.VMEM((2, NFFT, NFFT // 2), jnp.bfloat16),
            pltpu.VMEM((NFFT, MEL), jnp.bfloat16),
            pltpu.VMEM((width,), jnp.bfloat16),
            pltpu.VMEM((whole_width,), jnp.float32),
            pltpu.VMEM(rel_bias.shape, jnp.float32),
            pltpu.VMEM((heads, depth, width), jnp.bfloat16),
            pltpu.VMEM((heads, 1, width), jnp.float32),
            pltpu.VMEM((3, whole_width, width), jnp.bfloat16),
            pltpu.SMEM(utt_lengths.shape, jnp.int32),
            pltpu.VMEM((heads + 1, 4 * ROWS, MEL), jnp.float32),
            *[pltpu.VMEM((shards, cap, wide), jnp.bfloat16) for wide in payloads],
            *[pltpu.VMEM((shards, cap, wide), jnp.bfloat16) for wide in payloads],
            *[pltpu.VMEM((heads + 2, PE, wide), jnp.bfloat16) for wide in sizes],
            dma((12,)), dma((WAVE_CHUNKS,)),
            dma((SOLO + 1, others)), dma((SOLO + 1, others)),
            dma((others, groups - 1)), dma((others, groups - 1)),
            dma((others, groups + SOLO)), dma((others, groups + SOLO)),
            dma((COUNT, shards - 1)), dma((COUNT, shards - 1)),
            dma((COUNT, others)), dma((COUNT, others)),
            dma((COUNT, heads)), dma((COUNT,)), dma((others,)), dma((others,)), dma((2,)), dma((2,)),
        ],
        compiler_params=pltpu.CompilerParams(
            collective_id=0, has_side_effects=True, vmem_limit_bytes=36 << 20
        ),
        name="front",
    )(
        *[
            pltpu.with_memory_space_constraint(value, pltpu.HBM)
            for value in (
                wave_pieces.reshape(slots, samples),
                piece_target.reshape(1, slots),
                sub_weight,
                jnp.asarray(window_table()),
                jnp.asarray(fourier_tables()),
                jnp.asarray(mel_table()),
                sub_bias,
                norm_gain,
                rel_bias,
                jnp.transpose(qkv_weight, (1, 0, 2)),
                utt_lengths,
            )
        ]
    )

    return pl.pallas_call(
        back_kernel,
        out_shape=jax.ShapeDtypeStruct((tokens_here, width), jnp.bfloat16),
        in_specs=[vmem] * 4,
        out_specs=hbm,
        scratch_shapes=[
            pltpu.VMEM((tokens_here, width), jnp.bfloat16),
            dma((width // LANES,)),
        ],
        compiler_params=pltpu.CompilerParams(vmem_limit_bytes=24 << 20),
        name="back",
    )(queries, keys, values, position_bias)


def solution(mesh):
    placed = (
        P(("groups", "seq"), "head", "sub", None, None),
        P(("groups", "seq"), "head", "sub", None),
        P("groups"),
        P(None, "head"),
        P("head"),
        P(),
        P(None, None, "head"),
        P("head", None),
    )
    return jax.shard_map(
        functools.partial(
            local, mesh.shape["groups"], mesh.shape["seq"], mesh.shape["head"], mesh.shape["sub"]
        ),
        mesh=mesh,
        in_specs=placed,
        out_specs=P(("groups", "seq", "sub"), "head"),
        check_vma=False,
    )
```

```python
import functools
import math

import jax
import jax.numpy as jnp
import numpy as np
from jax import lax
from jax.experimental import pallas as pl
from jax.experimental.pallas import tpu as pltpu
from jax.sharding import PartitionSpec as P

HDIM = 64
MEL = 128
NFFT = 512
HOP = 160
FP = 17
CH = 136
PE = 32
LANES = 128
TABLE = 640
KEYS = 512
ROWS = 144


SAMPLE_RATE = 16000.0
EPSILON = 1e-05
MASKED = -1e30
MESH = pl.DeviceIdType.MESH


def split_bf16(table):
    high = table.astype(np.float32).astype(jnp.bfloat16)
    low = (table - high.astype(np.float64)).astype(np.float32).astype(jnp.bfloat16)
    return np.stack([high, low])


def window_table():
    return (0.5 - 0.5 * np.cos(2.0 * np.pi / NFFT * np.arange(NFFT)))[None].astype(np.float32)


def fourier_tables():
    half = NFFT // 2
    sample = np.arange(half)[:, None]

    def phase(bins):
        return (sample * bins[None, :] % NFFT) * (2.0 * np.pi / NFFT)

    even, odd = np.arange(0, half, 2), np.arange(1, half, 2)
    even_sine = np.sin(phase(even))
    even_sine[:, 0] = np.cos(phase(np.array([half])))[:, 0]
    even_table = np.concatenate([np.cos(phase(even)), even_sine], axis=1)
    odd_table = np.concatenate([np.cos(phase(odd)), np.sin(phase(odd))], axis=1)
    return np.stack([np.concatenate(split_bf16(t), axis=0) for t in (even_table, odd_table)])


def mel_table():
    bin_total = NFFT // 2 + 1
    highest = 2595.0 * math.log10(1.0 + SAMPLE_RATE / 2.0 / 700.0)
    points = np.arange(MEL + 2) * (highest / (MEL + 1))
    hertz = 700.0 * (np.power(10.0, points / 2595.0) - 1.0)
    centres = np.arange(bin_total) * (SAMPLE_RATE / NFFT)
    rising = (centres[:, None] - hertz[None, :-2]) / (hertz[1:-1] - hertz[:-2])[None, :]
    falling = (hertz[None, 2:] - centres[:, None]) / (hertz[2:] - hertz[1:-1])[None, :]
    table = np.maximum(0.0, np.minimum(rising, falling))
    sine_even = table[0 : bin_total - 1 : 2].copy()
    sine_even[0] = table[bin_total - 1]
    rows = np.concatenate(
        [table[0 : bin_total - 1 : 2], sine_even, table[1::2], table[1::2]], axis=0
    )
    return rows.astype(np.float32).astype(jnp.bfloat16)


def dot(left, right):
    return jnp.dot(left, right, preferred_element_type=jnp.float32)


def dot_split(value, table):
    value_high = value.astype(jnp.bfloat16)
    value_low = (value - value_high.astype(jnp.float32)).astype(jnp.bfloat16)
    depth = value.shape[1]
    table = jnp.concatenate([table[:depth], table[:depth], table[depth:]], axis=0)
    return dot(jnp.concatenate([value_high, value_low, value_high], axis=1), table)


PHASES = (
    (0, 1, 2, 3, 4, 5, 6, 7),
    (8, 9, 10, 11, 12, 13, 14, 15, 16),
)
COUNT = len(PHASES)
SOLO = 2
WAVE_CHUNKS = 3


def front_kernel(
    groups, shards, heads, subs,
    wave_in, target_in, weight_ref, window_in, fourier_in, mel_in, sub_bias_in, gain_in, rel_in,
    qkv_in, lengths_in,
    queries_ref, keys_ref, values_ref, bias_ref,
    wave_ref, target_ref, window_ref, fourier_ref, mel_ref, sub_bias_row, gain_row, rel_ref,
    weights_ref, sub_bias_ref, qkv_ref, lengths_ref, spread_ref,
    *rest,
):
    packed, received, frames = rest[:COUNT], rest[COUNT : 2 * COUNT], rest[2 * COUNT : 3 * COUNT]
    (
        lsem, vsem, wsend, wrecv, ysend, yrecv, fsend, frecv, asend, arecv, hsend, hrecv, nsend, nrecv,
        bsend, brecv, ksend, krecv,
    ) = rest[3 * COUNT :]
    mine = lax.axis_index("groups")
    s, h, u = lax.axis_index("seq"), lax.axis_index("head"), lax.axis_index("sub")
    half = s * subs + u
    halves = shards * subs
    slots = wave_ref.shape[0]
    cap = slots // shards
    depth = weight_ref.shape[0] // (subs * (groups + SOLO))

    def place_of(index, head):
        return {"seq": index // subs, "sub": index % subs, "head": head}

    def when(condition, action):
        @pl.when(condition)
        def _():
            action()

    pairs = (
        (target_in, target_ref), (window_in, window_ref), (fourier_in, fourier_ref),
        (mel_in, mel_ref), (sub_bias_in, sub_bias_row),
        (gain_in, gain_row), (rel_in, rel_ref), (lengths_in, lengths_ref),
        (weight_ref, weights_ref.at[h]),
        (qkv_in.at[0], qkv_ref.at[0]), (qkv_in.at[1], qkv_ref.at[1]),
        (qkv_in.at[2], qkv_ref.at[2]),
    )
    loads = [pltpu.make_async_copy(a, b, lsem.at[i]) for i, (a, b) in enumerate(pairs)]
    columns = wave_ref.shape[1] // WAVE_CHUNKS
    wave_loads = [
        pltpu.make_async_copy(
            wave_in.at[:, pl.ds(n * columns, columns)],
            wave_ref.at[:, pl.ds(n * columns, columns)],
            vsem.at[n],
        )
        for n in range(WAVE_CHUNKS)
    ]
    for load in loads[:3] + wave_loads + loads[3:8]:
        load.start()

    barrier = pltpu.get_barrier_semaphore()
    for d in range(1, shards):
        pl.semaphore_signal(
            barrier, inc=1, device_id={"seq": lax.rem(s + d, shards)}, device_id_type=MESH
        )
    for d in range(1, heads):
        pl.semaphore_signal(
            barrier, inc=1, device_id={"head": lax.rem(h + d, heads)}, device_id_type=MESH
        )

    for d in range(1, groups):
        pl.semaphore_signal(
            barrier, inc=1, device_id={"groups": lax.rem(mine + d, groups)}, device_id_type=MESH
        )

    sibling = {"sub": lax.rem(u + 1, subs)}
    pl.semaphore_signal(barrier, inc=1, device_id=sibling, device_id_type=MESH)
    far_up, far_down = (u != 0) & (half < halves - 1), (u == 0) & (half > 0)

    @pl.when(far_down)
    def _():
        pl.semaphore_signal(
            barrier, inc=1, device_id=place_of(half - 1, heads - 1), device_id_type=MESH
        )

    @pl.when(far_up)
    def _():
        pl.semaphore_signal(barrier, inc=1, device_id=place_of(half + 1, 0), device_id_type=MESH)

    def send_weights(source, owner, part, send_sem, recv_sem, device):
        rows = pl.ds((u * (groups + SOLO) + part) * depth, depth)
        copy = pltpu.make_async_remote_copy(
            src_ref=source.at[rows],
            dst_ref=weights_ref.at[owner, rows],
            send_sem=send_sem,
            recv_sem=recv_sem,
            device_id=device,
            device_id_type=MESH,
        )
        copy.start()
        return copy

    parts = [mine] + [groups + n for n in range(SOLO)]
    weight_copies, bias_copies = [], []
    loads[0].wait()
    target = target_ref[...]
    owner = jnp.where(target >= 0, lax.shift_right_arithmetic(target, 5), shards)
    place = jnp.bitwise_and(target, PE - 1)
    down = lax.broadcasted_iota(jnp.int32, (slots, slots), 0)
    across = lax.broadcasted_iota(jnp.int32, (slots, slots), 1)
    owner_wide = jnp.broadcast_to(owner, (slots, slots))
    owner_down = jnp.sum(jnp.where(down == across, owner_wide, 0), axis=1, keepdims=True)
    rank = jnp.sum(
        jnp.where((owner_down == owner_wide) & (down < across), 1, 0), axis=0, keepdims=True
    )
    goal = jnp.where(owner < shards, owner * cap + rank, -1)
    chosen = down == goal
    select = chosen.astype(jnp.float32).astype(jnp.bfloat16)
    code = jnp.sum(jnp.where(chosen, place + 1, 0), axis=1, keepdims=True).astype(jnp.float32)
    code = jnp.broadcast_to(code, (slots, LANES)).astype(jnp.bfloat16)

    piece_copies = []
    for index in range(1, 4):
        loads[index].wait()
    loaded = 0
    for phase, frame_numbers in enumerate(PHASES):
        pieces = []
        for f in frame_numbers:
            while loaded * columns < HOP * f + NFFT:
                wave_loads[loaded].wait()
                loaded += 1
            start = HOP * f // LANES * LANES
            if HOP * f == start:
                piece = wave_ref[:, start : start + NFFT]
            else:
                piece = wave_ref[:, start : start + NFFT + LANES]
                piece = pltpu.roll(piece, NFFT + LANES - (HOP * f - start), 1)[:, :NFFT]
            pieces.append(piece * window_ref[...])
        pieces = jnp.concatenate(pieces, axis=0)
        low, high = pieces[:, : NFFT // 2], pieces[:, NFFT // 2 :]
        even = dot_split(low + high, fourier_ref[0])
        odd = dot_split(low - high, fourier_ref[1])
        squares = jnp.concatenate([even * even, odd * odd], axis=1).astype(jnp.bfloat16)
        energy = dot(squares, mel_ref[...])
        logs = jnp.log(1.0 + energy).astype(jnp.bfloat16)
        count = len(frame_numbers)
        logs = jnp.concatenate([logs[n * slots : (n + 1) * slots] for n in range(count)], axis=1)
        rows = dot(select, logs).astype(jnp.bfloat16)
        for t in range(shards):
            packed[phase][t, :, : count * MEL] = rows[t * cap : (t + 1) * cap]
            if phase == 0:
                packed[0][t, :, count * MEL :] = code[t * cap : (t + 1) * cap]
        if phase == 0:
            edges = jnp.where((far_up & (h == heads - 1)) | (far_down & (h == 0)), heads, 0)
            pl.semaphore_wait(barrier, shards - 1 + heads - 1 + groups - 1 + 1 + edges)
            for n, part in enumerate(parts):
                for d in range(1, heads):
                    weight_copies.append(
                        send_weights(
                            weight_ref, h, part, wsend.at[n, d - 1], wrecv.at[n, d - 1],
                            {"head": lax.rem(h + d, heads)},
                        )
                    )
        for d in range(1, shards):
            to = lax.rem(s + d, shards)
            copy = pltpu.make_async_remote_copy(
                src_ref=packed[phase].at[to],
                dst_ref=received[phase].at[s],
                send_sem=asend.at[phase, d - 1],
                recv_sem=arecv.at[phase, d - 1],
                device_id={"seq": to},
                device_id_type=MESH,
            )
            copy.start()
            piece_copies.append(copy)
        received[phase][s] = packed[phase][s]

    for load in loads[8:]:
        load.start()
    loads[4].wait()
    sub_bias_ref[h] = sub_bias_row[...].astype(jnp.float32).reshape(1, sub_bias_row.shape[0])
    for d in range(1, heads):
        copy = pltpu.make_async_remote_copy(
            src_ref=sub_bias_ref.at[h],
            dst_ref=sub_bias_ref.at[h],
            send_sem=bsend.at[d - 1],
            recv_sem=brecv.at[d - 1],
            device_id={"head": lax.rem(h + d, heads)},
            device_id_type=MESH,
        )
        copy.start()
        bias_copies.append(copy)

    across_copies, forward_copies = [], []

    def forward(source, part, d, index):
        forward_copies.append(
            send_weights(
                weights_ref.at[source], source, part,
                fsend.at[d - 1, index], frecv.at[d - 1, index], sibling,
            )
        )

    def spread_weights(n):
        for d in range(1, heads):
            source = lax.rem(h - d + heads, heads)
            weight_copies[n * (heads - 1) + d - 1].wait_recv()
            if n == 0:
                for e in range(1, groups):
                    across_copies.append(
                        send_weights(
                            weights_ref.at[source], source, mine,
                            ysend.at[d - 1, e - 1], yrecv.at[d - 1, e - 1],
                            {"groups": lax.rem(mine + e, groups)},
                        )
                    )
            forward(source, parts[n], d, n)

    def forward_weights():
        for d in range(1, heads):
            source = lax.rem(h - d + heads, heads)
            for e in range(1, groups):
                across_copies[(d - 1) * (groups - 1) + e - 1].wait_recv()
                forward(source, lax.rem(mine - e + groups, groups), d, SOLO + e)

    def clear(start, count):
        for out in (keys_ref, values_ref):
            out[start : start + count, :] = jnp.zeros((count, out.shape[1]), jnp.bfloat16)

    last = (heads + 1) * ROWS
    when(half == 0, lambda: clear(0, ROWS))
    when(half == halves - 1, lambda: clear(last, ROWS))
    clear(last + ROWS, keys_ref.shape[0] - last - ROWS)

    for slot in range(spread_ref.shape[0]):
        spread_ref[slot, PE * FP :] = jnp.zeros((4 * ROWS - PE * FP, MEL), jnp.float32)

    for index in range(5, 8):
        loads[index].wait()
    first_token, token_total = half * heads * CH, halves * heads * CH
    masks = []
    for b in range(heads):
        query_pos = first_token + b * CH + lax.broadcasted_iota(jnp.int32, (CH, 1), 0)
        key_index = lax.broadcasted_iota(jnp.int32, (1, KEYS), 1)
        gap = jnp.zeros_like(key_index)
        for e in range(1, 4):
            gap = gap + (key_index >= e * ROWS).astype(jnp.int32)
        key_in = key_index - gap * ROWS
        key_pos = first_token + (b - 1 + gap) * CH + key_in
        end = jnp.int32(0)
        query_utt = jnp.zeros_like(query_pos)
        key_utt = jnp.zeros_like(key_pos)
        for r in range(lengths_ref.shape[0]):
            end = end + lengths_ref[r]
            query_utt = query_utt + (query_pos >= end).astype(jnp.int32)
            key_utt = key_utt + (key_pos >= end).astype(jnp.int32)
        inside = (key_pos >= 0) & (key_pos < token_total) & (gap < 3) & (key_in < CH)
        key_utt = jnp.where(inside, key_utt, -1)
        masks.append(jnp.where(query_utt == key_utt, 0.0, MASKED))
    taps = rel_ref.shape[1]
    mirror = lax.broadcasted_iota(jnp.int32, (taps, TABLE), 0) + lax.broadcasted_iota(
        jnp.int32, (taps, TABLE), 1
    )
    mirror = (mirror == taps - 1).astype(jnp.float32).astype(jnp.bfloat16)
    rest = rel_ref[...]
    terms = []
    for _ in range(3):
        term = rest.astype(jnp.bfloat16)
        rest = rest - term.astype(jnp.float32)
        terms.append(dot(term, mirror))
    key_lane = lax.broadcasted_iota(jnp.int32, (1, KEYS), 1)
    flipped = terms[0] + (terms[1] + terms[2])
    for row in range(rel_ref.shape[0]):
        wide = jnp.broadcast_to(flipped[row : row + 1, :], (CH, TABLE))
        wide = pltpu.roll(wide, TABLE - (CH - 1), 1, stride=1, stride_axis=0)
        once = pltpu.roll(wide, ROWS - CH, 1)[:, :KEYS]
        twice = pltpu.roll(wide, 2 * (ROWS - CH), 1)[:, :KEYS]
        spaced = jnp.where(
            key_lane < ROWS, wide[:, :KEYS], jnp.where(key_lane < 2 * ROWS, once, twice)
        )
        for b in range(heads):
            bias_ref[row, b] = spaced + masks[b]
        if row + 1 == rel_ref.shape[0] * 2 // 3:
            spread_weights(0)

    spread_weights(1)
    head_copies = []

    def send_heads(phase):
        for d in range(1, heads):
            copy = pltpu.make_async_remote_copy(
                src_ref=frames[phase].at[h + 1],
                dst_ref=frames[phase].at[h + 1],
                send_sem=hsend.at[phase, d - 1],
                recv_sem=hrecv.at[phase, d - 1],
                device_id={"head": lax.rem(h + d, heads)},
                device_id_type=MESH,
            )
            copy.start()
            head_copies.append(copy)

    def halo(to, head, source, row, phase):
        return pltpu.make_async_remote_copy(
            src_ref=frames[phase].at[source],
            dst_ref=frames[phase].at[row],
            send_sem=nsend.at[phase, head],
            recv_sem=nrecv.at[phase],
            device_id=place_of(to, head),
            device_id_type=MESH,
        )

    def halo_up(head, phase):
        return halo(half + 1, head, heads, 0, phase)

    def halo_down(head, phase):
        return halo(half - 1, head, 1, heads + 1, phase)

    def send_far(phase):
        def up():
            for head in range(heads - 1, -1, -1):
                halo_up(head, phase).start()

        def down():
            for head in range(heads):
                halo_down(head, phase).start()

        when(far_up & (h == heads - 1), up)
        when(far_down & (h == 0), down)

    def arrive(phase):
        for d in range(1, shards):
            piece_copies[phase * (shards - 1) + d - 1].wait_recv()
        arrived = received[phase][...]
        if cap % 16:
            arrived = arrived.astype(jnp.float32).reshape(slots, arrived.shape[2])
            return arrived.astype(jnp.bfloat16)
        return arrived.reshape(slots, arrived.shape[2])

    def lay(eighth, slot, phases):
        for phase in phases:
            block = frames[phase][eighth].astype(jnp.float32)
            for n, f in enumerate(PHASES[phase]):
                spread_ref[slot, pl.ds(f, PE, stride=FP), :] = block[:, n * MEL : (n + 1) * MEL]

    early, late = range(COUNT - 1), (COUNT - 1,)

    order = None
    for phase, frame_numbers in enumerate(PHASES):
        if phase == COUNT - 1:
            for n in range(2, SOLO + 1):
                spread_weights(n)
        arrived = arrive(phase)
        wide = len(frame_numbers) * MEL
        if order is None:
            code_down = arrived[:, wide : wide + 1].astype(jnp.float32)
            code_wide = jnp.broadcast_to(code_down, (slots, slots))
            code_across = jnp.sum(jnp.where(down == across, code_wide, 0.0), axis=0, keepdims=True)
            piece = lax.broadcasted_iota(jnp.int32, (PE, slots), 0).astype(jnp.float32) + 1.0
            order = (piece == code_across).astype(jnp.float32).astype(jnp.bfloat16)
        frames[phase][h + 1] = dot(order, arrived[:, :wide]).astype(jnp.bfloat16)
        send_heads(phase)
        if phase < COUNT - 1:
            send_far(phase)
            lay(h + 1, 0, (phase,))

    forward_weights()
    for copy in forward_copies + bias_copies:
        copy.wait_recv()
    loads[8].wait()

    def normed_tokens(slot):
        spread = spread_ref.at[slot]
        tokens = jnp.concatenate(
            [spread[pl.ds(m, ROWS, stride=4), :] for m in range(4)], axis=1
        ).astype(jnp.bfloat16)
        summed = jnp.concatenate(
            [dot(tokens, weights_ref[g]) + sub_bias_ref[g] for g in range(heads)], axis=1
        )
        value = (summed / (1.0 + jnp.exp(-summed))).astype(jnp.bfloat16).astype(jnp.float32)
        mean = jnp.mean(value, axis=1, keepdims=True)
        centred = value - mean
        variance = jnp.mean(centred * centred, axis=1, keepdims=True)
        gain = gain_row[...].reshape(1, gain_row.shape[0])
        return (centred * lax.rsqrt(variance + EPSILON) * gain).astype(jnp.bfloat16)

    def project(eighth, normed, own):
        if own:
            rows = pl.ds(pl.multiple_of((eighth - 1) * CH, 8), CH)
            queries_ref[rows, :] = dot(normed, qkv_ref[0])[:CH] * (1.0 / math.sqrt(HDIM))
        rows = pl.ds(pl.multiple_of(eighth * ROWS, ROWS), ROWS)
        keys_ref[rows, :] = dot(normed, qkv_ref[1]).astype(jnp.bfloat16)
        values_ref[rows, :] = dot(normed, qkv_ref[2]).astype(jnp.bfloat16)

    edge = jnp.where(u == 0, heads, 1)
    source_rows = pl.ds(pl.multiple_of(edge * ROWS, ROWS), ROWS)
    landing = pl.ds(pl.multiple_of(jnp.where(u == 0, 0, heads + 1) * ROWS, ROWS), ROWS)
    edge_copies = [
        pltpu.make_async_remote_copy(
            src_ref=out.at[source_rows],
            dst_ref=out.at[landing],
            send_sem=ksend.at[index],
            recv_sem=krecv.at[index],
            device_id=sibling,
            device_id_type=MESH,
        )
        for index, out in enumerate((keys_ref, values_ref))
    ]

    def send_edge():
        for copy in edge_copies:
            copy.start()

    lay(h + 1, 0, late)
    normed = normed_tokens(0)
    send_far(COUNT - 1)
    for index in range(9, 12):
        loads[index].wait()
    project(h + 1, normed, True)
    when(edge == h + 1, send_edge)
    for copy in bias_copies + weight_copies + across_copies + forward_copies + piece_copies:
        copy.wait_send()
    far_row = jnp.where(u == 0, 0, heads + 1)

    def far_early():
        for phase in early:
            halo(0, 0, 1, far_row, phase).wait_recv()
        lay(far_row, heads, early)

    def far_late():
        for phase in late:
            halo(0, 0, 1, far_row, phase).wait_recv()
        lay(far_row, heads, late)
        project(far_row, normed_tokens(heads), False)

    def wait_heads(d, phases):
        other = lax.rem(h - d + heads, heads) + 1
        for phase in phases:
            head_copies[phase * (heads - 1) + d - 1].wait_recv()
        lay(other, d, phases)
        return other

    when(far_up | far_down, far_early)
    for d in range(1, heads):
        wait_heads(d, early)
    for d in range(1, heads):
        other = wait_heads(d, late)
        project(other, normed_tokens(d), True)
        when(edge == other, send_edge)
    when(far_up | far_down, far_late)

    for copy in edge_copies:
        copy.wait()
    for copy in head_copies:
        copy.wait_send()

    def far_sent(send):
        for phase in range(COUNT):
            for head in range(heads):
                send(head, phase).wait_send()

    when(far_up & (h == heads - 1), lambda: far_sent(halo_up))
    when(far_down & (h == 0), lambda: far_sent(halo_down))


def back_kernel(queries, keys, values, bias_ref, context_out, context_ref, sem):
    blocks = bias_ref.shape[1]
    width = queries.shape[1]
    lane = lax.broadcasted_iota(jnp.int32, (1, LANES), 1)
    ones = jnp.ones((KEYS, LANES), jnp.bfloat16)
    copies = []
    for pair in range(width // LANES):
        lanes = slice(pair * LANES, (pair + 1) * LANES)
        for b in range(blocks):
            query = queries[b * CH : (b + 1) * CH, lanes]
            key = keys[b * ROWS : b * ROWS + KEYS, lanes]
            value = values[b * ROWS : b * ROWS + KEYS, lanes]
            both = jnp.concatenate(
                [jnp.where(lane < HDIM, query, 0.0), jnp.where(lane < HDIM, 0.0, query)], axis=0
            ).astype(jnp.bfloat16)
            scores = lax.dot_general(
                both, key, (((1,), (1,)), ((), ())), preferred_element_type=jnp.float32
            )
            shift = jnp.concatenate([bias_ref[2 * pair, b], bias_ref[2 * pair + 1, b]], axis=0)
            scores = scores + shift
            raised = jnp.exp(scores - jnp.max(scores, axis=1, keepdims=True)).astype(jnp.bfloat16)
            out = dot(raised, jnp.concatenate([value, ones], axis=1))
            out = jnp.where(
                jnp.concatenate([lane, lane], axis=1) % LANES < HDIM, out[:CH], out[CH:]
            )
            joined = out[:, :LANES] / out[:, LANES:]
            context_ref[b * CH : (b + 1) * CH, lanes] = joined.astype(jnp.bfloat16)
        copy = pltpu.make_async_copy(
            context_ref.at[:, lanes], context_out.at[:, lanes], sem.at[pair]
        )
        copy.start()
        copies.append(copy)
    for copy in copies:
        copy.wait()


def local(
    groups, shards, heads, subs,
    wave_pieces, piece_target, utt_lengths, sub_weight, sub_bias, norm_gain, qkv_weight, rel_bias,
):
    slots, samples = wave_pieces.shape[3:]
    cap = slots // shards
    depth, width = sub_weight.shape
    whole_width = qkv_weight.shape[0]
    vmem = pl.BlockSpec(memory_space=pltpu.VMEM)
    sizes = [len(frame_numbers) * MEL for frame_numbers in PHASES]
    payloads = [size + (phase == 0) * MEL for phase, size in enumerate(sizes)]
    dma = pltpu.SemaphoreType.DMA
    hbm = pl.BlockSpec(memory_space=pltpu.HBM)
    heads_here = rel_bias.shape[0]
    tokens_here = heads * CH
    key_rows = (heads - 1) * ROWS + KEYS
    others = heads - 1
    queries, keys, values, position_bias = pl.pallas_call(
        functools.partial(front_kernel, groups, shards, heads, subs),
        out_shape=(
            jax.ShapeDtypeStruct((tokens_here, width), jnp.float32),
            jax.ShapeDtypeStruct((key_rows, width), jnp.bfloat16),
            jax.ShapeDtypeStruct((key_rows, width), jnp.bfloat16),
            jax.ShapeDtypeStruct((heads_here, heads, CH, KEYS), jnp.float32),
        ),
        in_specs=[hbm] * 11,
        out_specs=(vmem,) * 4,
        scratch_shapes=[
            pltpu.VMEM((slots, samples), jnp.float32),
            pltpu.VMEM((1, slots), jnp.int32),
            pltpu.VMEM((1, NFFT), jnp.float32),
            pltpu.VMEM((2, NFFT, NFFT // 2), jnp.bfloat16),
            pltpu.VMEM((NFFT, MEL), jnp.bfloat16),
            pltpu.VMEM((width,), jnp.bfloat16),
            pltpu.VMEM((whole_width,), jnp.float32),
            pltpu.VMEM(rel_bias.shape, jnp.float32),
            pltpu.VMEM((heads, depth, width), jnp.bfloat16),
            pltpu.VMEM((heads, 1, width), jnp.float32),
            pltpu.VMEM((3, whole_width, width), jnp.bfloat16),
            pltpu.SMEM(utt_lengths.shape, jnp.int32),
            pltpu.VMEM((heads + 1, 4 * ROWS, MEL), jnp.float32),
            *[pltpu.VMEM((shards, cap, wide), jnp.bfloat16) for wide in payloads],
            *[pltpu.VMEM((shards, cap, wide), jnp.bfloat16) for wide in payloads],
            *[pltpu.VMEM((heads + 2, PE, wide), jnp.bfloat16) for wide in sizes],
            dma((12,)), dma((WAVE_CHUNKS,)),
            dma((SOLO + 1, others)), dma((SOLO + 1, others)),
            dma((others, groups - 1)), dma((others, groups - 1)),
            dma((others, groups + SOLO)), dma((others, groups + SOLO)),
            dma((COUNT, shards - 1)), dma((COUNT, shards - 1)),
            dma((COUNT, others)), dma((COUNT, others)),
            dma((COUNT, heads)), dma((COUNT,)), dma((others,)), dma((others,)), dma((2,)), dma((2,)),
        ],
        compiler_params=pltpu.CompilerParams(
            collective_id=0, has_side_effects=True, vmem_limit_bytes=36 << 20
        ),
        name="front",
    )(
        *[
            pltpu.with_memory_space_constraint(value, pltpu.HBM)
            for value in (
                wave_pieces.reshape(slots, samples),
                piece_target.reshape(1, slots),
                sub_weight,
                jnp.asarray(window_table()),
                jnp.asarray(fourier_tables()),
                jnp.asarray(mel_table()),
                sub_bias,
                norm_gain,
                rel_bias,
                jnp.transpose(qkv_weight, (1, 0, 2)),
                utt_lengths,
            )
        ]
    )

    return pl.pallas_call(
        back_kernel,
        out_shape=jax.ShapeDtypeStruct((tokens_here, width), jnp.bfloat16),
        in_specs=[vmem] * 4,
        out_specs=hbm,
        scratch_shapes=[
            pltpu.VMEM((tokens_here, width), jnp.bfloat16),
            dma((width // LANES,)),
        ],
        compiler_params=pltpu.CompilerParams(vmem_limit_bytes=24 << 20),
        name="back",
    )(queries, keys, values, position_bias)


def solution(mesh):
    placed = (
        P(("groups", "seq"), "head", "sub", None, None),
        P(("groups", "seq"), "head", "sub", None),
        P("groups"),
        P(None, "head"),
        P("head"),
        P(),
        P(None, None, "head"),
        P("head", None),
    )
    return jax.shard_map(
        functools.partial(
            local, mesh.shape["groups"], mesh.shape["seq"], mesh.shape["head"], mesh.shape["sub"]
        ),
        mesh=mesh,
        in_specs=placed,
        out_specs=P(("groups", "seq", "sub"), "head"),
        check_vma=False,
    )
```
